128 devices in a mesh: sx: 4 (over y_hi, core), sy: 16 (over z, x), depth: 2 (over y_lo).
Axes of the slice: x: 4, y: 4 (y_hi: 2, y_lo: 2; y = y_hi * 2 + y_lo), z: 4, core: 2. Of those that a mesh axis runs over, the one named last changes fastest.
Arguments:
- probe_wave: float32 [2, 128, 128], replicated, may hold values from -4.2 to 4.2
- transmission: float32 [2, 8, 512, 4096], P(None, 'depth', 'sx', 'sy'), may hold values from -0.6 to 0.6
- scan_offsets: int32 [4, 16, 4, 2], P('sx', 'sy'), may hold values from -64 to 192, as said below
- pattern_shifts: int32 [4, 16, 4, 2], P('sx', 'sy'), may hold values from -8 to 8
- patterns: float32 [4, 16, 4, 128, 128], P('sx', 'sy'), may hold values from 0 to 9
Outputs:
- transmission_grad: float32 [2, 8, 512, 4096], P(None, 'depth', 'sx', 'sy')
- probe_grad: float32 [2, 128, 128], replicated
- mean_error: float32 [], replicated
The draws below stay inside these ranges and needn't reach their ends.
Inputs may be any that keep to these rules, and one draw needn't show every extreme that they name: `scan_offsets`: row offsets lie from -64 to 64 and column offsets from -64 to 192; on every scan tile some position takes the smallest and some the largest value of each.
All inputs are finite; a program needn't handle non-finite values.
Results may differ from the reference program's by a relative error of at most 0.0003.
Values sent between devices are 32-bit elements; how exact they have to be, the bound alone decides.
No kernel may reach another device: no remote copies, remote signals or barrier semaphores. Data moves between devices by JAX's collectives and lax.ppermute only.
A program may use at most 64 MiB of HBM per device.

```python
import jax
import jax.numpy as jnp
from jax import lax

WIN = 128
POS_DEV = 4
TILE_R = 128
TILE_C = 256
SLABS = 8
HALF = 64
NROW = 512
NCOL = 4096
POSITIONS = 256
N_SX = 4
N_SY = 16


def draw_scan_offsets(key, part):
    keyed = jax.random.fold_in(key, 7)
    first_key, second_key, third_key, fourth_key = jax.random.split(keyed, 4)
    extent = (N_SX, N_SY, POS_DEV)
    row_values = jax.random.randint(first_key, extent, -HALF, TILE_R - HALF + 1)
    col_values = jax.random.randint(second_key, extent, -HALF, TILE_C - HALF + 1)
    lowest = jax.random.randint(third_key, (N_SX, N_SY, 1), 0, POS_DEV)
    offset_step = jax.random.randint(fourth_key, (N_SX, N_SY, 1), 1, POS_DEV)
    highest = (lowest + offset_step) % POS_DEV
    counter = jnp.arange(POS_DEV, dtype=jnp.int32)[None, None, :]
    row_values = jnp.where(counter == lowest, -HALF, row_values)
    row_values = jnp.where(counter == highest, TILE_R - HALF, row_values)
    col_values = jnp.where(counter == lowest, -HALF, col_values)
    col_values = jnp.where(counter == highest, TILE_C - HALF, col_values)
    return jnp.stack([row_values, col_values], axis=-1).astype(jnp.int32)


def draw_patterns(key, part):
    keyed = jax.random.fold_in(key, 11)
    extent = (N_SX, N_SY, POS_DEV, WIN, WIN)
    tile_index = jnp.arange(N_SX * N_SY, dtype=jnp.int32).reshape(N_SX, N_SY, 1, 1, 1).astype(jnp.float32)
    growth = 1.0 + 2.0 * tile_index / max(N_SX * N_SY - 1, 1)
    values = jax.random.uniform(keyed, extent, jnp.float32, 0.0, 2.0)
    return values * growth


def touch_ends(drawn, key, low, top_value):
    shape = drawn.shape
    spot = [jax.random.randint(jax.random.fold_in(key, axis), (), 0, shape[axis]) for axis in range(len(shape))]
    drawn = drawn.at[tuple(spot)].set(low)
    longest = shape.index(max(shape))
    spot[longest] = (spot[longest] + 1) % shape[longest]
    return drawn.at[tuple(spot)].set(top_value)


def steps_of(key, shape, cuts, smallest, top_value):
    factor_of = 1.0
    for axis_at, parts in cuts:
        steps = jax.random.uniform(jax.random.fold_in(jax.random.fold_in(key, 6), axis_at), (parts,), jnp.float32, smallest / len(cuts), top_value / len(cuts))
        factor_of = factor_of * jnp.repeat(jnp.exp(steps), shape[axis_at] // parts).reshape((-1,) + (1,) * (len(shape) - 1 - axis_at))
    return factor_of


def bell_draw(rng, dims, deviation, reach, cuts=(), kind=jnp.bfloat16):
    gain = steps_of(rng, dims, cuts, -0.22, 0.18) if cuts else 1.0
    drawn = jax.random.normal(rng, dims, jnp.float32) * deviation * gain
    return jnp.minimum(jnp.maximum(drawn, -reach), reach).astype(kind)


def setup_inputs(seed: int = 0) -> dict:
    arg_keys = jax.random.split(jax.random.key(seed), 6)
    return {
        "probe_wave": bell_draw(arg_keys[0], (2, WIN, WIN), 0.7, 4.2, (), jnp.float32),
        "transmission": bell_draw(arg_keys[1], (2, SLABS, NROW, NCOL), 0.1, 0.6, ((1, 2), (2, 4), (3, 16)), jnp.float32),
        "scan_offsets": draw_scan_offsets(jax.random.fold_in(arg_keys[5], 71), 0),
        "pattern_shifts": touch_ends(jax.random.randint(arg_keys[3], (N_SX, N_SY, POS_DEV, 2), -8, 9), jax.random.fold_in(arg_keys[3], 1), -8, 8).astype(jnp.int32),
        "patterns": draw_patterns(jax.random.fold_in(arg_keys[5], 71), 0),
    }


FRESNEL = 12.0

def propagate(incoming, kernel):
    return jnp.fft.ifft2(jnp.fft.fft2(incoming) * kernel)

def position_error(windows, probe_wave, measured, shift_pair, kernel):
    current = lax.complex(probe_wave[0], probe_wave[1])
    for slab_number in range(windows.shape[1]):
        factor_layer = lax.complex(1.0 + windows[0, slab_number], windows[1, slab_number])
        current = propagate(current * factor_layer, kernel)
    detector = jnp.fft.fft2(current, norm='ortho')
    intensity = jnp.real(detector) ** 2 + jnp.imag(detector) ** 2
    moved = jnp.roll(intensity, (shift_pair[0], shift_pair[1]), axis=(0, 1))
    residual = moved - measured
    return 0.5 * jnp.sum(residual * residual)

def reference(probe_wave, transmission, scan_offsets, pattern_shifts, patterns):
    border = WIN // 2
    counter = jnp.arange(WIN, dtype=jnp.int32)
    frequency = jnp.where(counter < WIN // 2, counter, counter - WIN).astype(jnp.float32) / WIN
    phases = -FRESNEL * (frequency[:, None] ** 2 + frequency[None, :] ** 2)
    kernel = lax.complex(jnp.cos(phases), jnp.sin(phases))
    grid_rows = jnp.arange(N_SX, dtype=jnp.int32)[:, None, None] * TILE_R
    grid_cols = jnp.arange(N_SY, dtype=jnp.int32)[None, :, None] * TILE_C
    row_starts = (scan_offsets[..., 0] + grid_rows + border).reshape(-1).astype(jnp.int32)
    col_starts = (scan_offsets[..., 1] + grid_cols + border).reshape(-1).astype(jnp.int32)
    shift_table = pattern_shifts.reshape(-1, 2)
    measured_all = patterns.reshape(-1, WIN, WIN)
    padded = jnp.pad(transmission, ((0, 0), (0, 0), (border, border), (border, border)))
    zero_index = jnp.zeros((), jnp.int32)

    def advance(running, inputs):
        gradients, probe_total, error_total = running
        row_start, col_start, shift_pair, measured = inputs
        corner = (zero_index, zero_index, row_start, col_start)
        windows = lax.dynamic_slice(padded, corner, (2, SLABS, WIN, WIN))

        def local_error(window_values, probe_values):
            return position_error(window_values, probe_values, measured, shift_pair, kernel)
        amount, pullback = jax.vjp(local_error, windows, probe_wave)
        window_grad, probe_part = pullback(jnp.ones_like(amount))
        current = lax.dynamic_slice(gradients, corner, (2, SLABS, WIN, WIN))
        gradients = lax.dynamic_update_slice(gradients, current + window_grad, corner)
        return ((gradients, probe_total + probe_part, error_total + amount), None)
    initial = (jnp.zeros(padded.shape, jnp.float32), jnp.zeros((2, WIN, WIN), jnp.float32), jnp.zeros((), jnp.float32))
    final, _ = lax.scan(advance, initial, (row_starts, col_starts, shift_table, measured_all))
    gradients, probe_total, error_total = final
    transmission_grad = gradients[:, :, border:border + NROW, border:border + NCOL]
    return (transmission_grad, probe_total / POSITIONS, error_total / (POSITIONS * WIN * WIN))
```

```python
import functools

import jax
import jax.numpy as jnp
import numpy as np
from jax import lax
from jax.experimental import pallas as pl
from jax.experimental.pallas import tpu as pltpu
from jax.sharding import PartitionSpec as P

FRESNEL = 12.0
WIN = 128
HALF = 64
TALL = WIN + 8
F32 = jnp.float32
BF16 = jnp.bfloat16
VMEM_LIMIT = 56 * 1024 * 1024


def tables():
    n = np.arange(WIN)
    fourier = np.exp(-2j * np.pi * (np.outer(n, n) % WIN) / WIN) / np.sqrt(WIN)
    freq = np.where(n < WIN // 2, n, n - WIN) / WIN
    phase = np.exp(-1j * FRESNEL * freq * freq)
    prop = fourier.conj() @ (phase[:, None] * fourier)
    exit_left = fourier @ prop
    exit_right = prop @ fourier
    return prop, exit_left, exit_right


def right_block(m):
    return np.block([[m.real, m.imag], [-m.imag, m.real]])


def left_block(m):
    return np.block([[m.real, -m.imag], [m.imag, m.real]])


def halves(m):
    m = m.astype(np.float32)
    hi = m.astype(jnp.bfloat16)
    lo = (m - hi.astype(np.float32)).astype(jnp.bfloat16)
    return np.stack([hi, lo])


def constants():
    prop, exit_left, exit_right = tables()
    steps = np.stack([halves(right_block(prop)), halves(left_block(prop))])
    exits = np.stack([halves(right_block(exit_right)), halves(left_block(exit_left))])
    return jnp.asarray(steps), jnp.asarray(exits)


def split(x):
    hi = x.astype(BF16)
    return hi, (x - hi.astype(F32)).astype(BF16)


def mm(a, b):
    return jnp.dot(a, b, preferred_element_type=F32)


def mm3(a, b):
    return mm(a[0], b[0]) + (mm(a[1], b[0]) + mm(a[0], b[1]))


def apply_both(fields, right, left):
    rows = jnp.concatenate([jnp.concatenate([re, im], axis=1) for re, im in fields], axis=0)
    z = mm3(split(rows), right)
    cols = jnp.concatenate(
        [
            jnp.concatenate([z[p * WIN : (p + 1) * WIN, :WIN], z[p * WIN : (p + 1) * WIN, WIN:]], axis=0)
            for p in range(len(fields))
        ],
        axis=1,
    )
    y = mm3(left, split(cols))
    return [
        (y[:WIN, p * WIN : (p + 1) * WIN], y[WIN:, p * WIN : (p + 1) * WIN]) for p in range(len(fields))
    ]


def times(a, b):
    return a[0] * b[0] - a[1] * b[1], a[0] * b[1] + a[1] * b[0]


def conj_times(a, b):
    return a[0] * b[0] + a[1] * b[1], a[0] * b[1] - a[1] * b[0]


def pair(ref, i):
    return ref[i, 0], ref[i, 1]


def roll_half(x):
    return pltpu.roll(x, HALF, axis=x.ndim - 1)


def join(low, high):
    lane = lax.broadcasted_iota(jnp.int32, low.shape, low.ndim - 1)
    return jnp.where(lane < HALF, low, high)


def pack_columns_kernel(pos, tile, first, second):
    right = join(roll_half(tile[0, :, :, 128:]), tile[1, :, :, 128:])
    left = join(tile[0, :, :, :128], roll_half(tile[1, :, :, :128]))
    even = pos[1] == 0

    @pl.when(even)
    def _():
        first[...] = right
        second[...] = left

    @pl.when(jnp.logical_not(even))
    def _():
        first[...] = left
        second[...] = right


def pack_rows_kernel(pos, tile, col1, col2, first, second):
    even = pos[1] == 0

    def put(out, start):
        rows = pl.ds(pl.multiple_of(start, 64), 64)
        out[:, :, 0:256] = tile[0, :, rows, :]
        out[:, :, 256:512] = tile[1, :, rows, :]

        @pl.when(even)
        def _():
            out[:, :, 512:640] = col2[:, rows, :]
            out[:, :, 640:768] = col1[:, rows, :]

        @pl.when(jnp.logical_not(even))
        def _():
            out[:, :, 512:640] = col1[:, rows, :]
            out[:, :, 640:768] = col2[:, rows, :]

    low = pos[2] * 64
    put(first, 64 - low)
    put(second, low)


def load_window(ext, c, k, row, block, shift):
    base = pl.multiple_of(row // 8 * 8, 8)
    wide = ext[c, k, pl.ds(base, TALL), pl.ds(pl.multiple_of(block * 128, 128), 256)]
    wide = pltpu.roll(wide, (256 - shift) & 255, axis=1)[:, :WIN]
    return pltpu.roll(wide, (TALL - row % 8) % TALL, axis=0)[:WIN]


def place(offs, p):
    row = offs[p, 0] + HALF
    col = offs[p, 1] + 128
    return row, col // 128, col % 128


def forward_kernel(count, pos, offs, probe, tile, col1, col2, row1, row2, mats, wave, win, psi, ext):
    slabs = tile.shape[1]
    even_col = pos[1] == 0
    ext[:, :, 64:192, 128:384] = tile[...]

    def columns(left, right):
        ext[0, :, 64:192, 0:128] = roll_half(left[...])
        ext[1, :, 64:192, 0:128] = left[...]
        ext[0, :, 64:192, 384:512] = right[...]
        ext[1, :, 64:192, 384:512] = roll_half(right[...])

    @pl.when(even_col)
    def _():
        columns(col2, col1)

    @pl.when(jnp.logical_not(even_col))
    def _():
        columns(col1, col2)

    def rim(ref, start):
        rows = pl.ds(pl.multiple_of(start, 64), 64)
        ext[0, :, rows, 128:384] = ref[:, :, 0:256]
        ext[1, :, rows, 128:384] = ref[:, :, 256:512]
        left = ref[:, :, 512:640]
        right = ref[:, :, 640:768]
        ext[0, :, rows, 0:128] = roll_half(left)
        ext[1, :, rows, 0:128] = left
        ext[0, :, rows, 384:512] = right
        ext[1, :, rows, 384:512] = roll_half(right)

    odd_row = pos[2]
    rim(row1, 192 * (1 - odd_row))
    rim(row2, 192 * odd_row)

    for p in range(count):
        row, block, shift = place(offs, p)
        for k in range(slabs):
            win[k, p, 0] = load_window(ext, 0, k, row, block, shift) + 1.0
            win[k, p, 1] = load_window(ext, 1, k, row, block, shift)

    @pl.when(pos[0] == 0)
    def _():
        right = (mats[0, 0], mats[0, 1])
        left = (mats[1, 0], mats[1, 1])
        fields = [(probe[0], probe[1])] * count
        for k in range(slabs):
            if k:
                for p in range(count):
                    psi[k - 1, p, 0], psi[k - 1, p, 1] = fields[p]
            fields = apply_both([times(fields[p], pair(win.at[k], p)) for p in range(count)], right, left)
        for p in range(count):
            wave[p, 0], wave[p, 1] = fields[p]


def add_window(ext, c, k, row, block, shift, piece):
    tall = pltpu.roll(jnp.concatenate([piece, jnp.zeros((TALL - WIN, WIN), F32)], axis=0), row % 8, axis=0)
    wide = pltpu.roll(jnp.concatenate([tall, jnp.zeros_like(tall)], axis=1), shift, axis=1)
    base = pl.multiple_of(row // 8 * 8, 8)
    at = (c, k, pl.ds(base, TALL), pl.ds(pl.multiple_of(block * 128, 128), 256))
    ext[at] = ext[at] + wide


def emit_gradient(pos, ext, center, first, second, strip_l, strip_r):
    center[...] = ext[:, :, 64:192, 128:384]

    def strip(rows):
        left = join(roll_half(ext[0, :, rows, 0:128]), ext[1, :, rows, 0:128])
        right = join(ext[0, :, rows, 384:512], roll_half(ext[1, :, rows, 384:512]))
        return left, right

    strip_l[...], strip_r[...] = strip(slice(64, 192))

    def rim(out, start):
        rows = pl.ds(pl.multiple_of(start, 64), 64)
        out[:, :, 0:256] = ext[0, :, rows, 128:384]
        out[:, :, 256:512] = ext[1, :, rows, 128:384]
        out[:, :, 512:640], out[:, :, 640:768] = strip(rows)

    odd_row = pos[2]
    rim(first, 192 * (1 - odd_row))
    rim(second, 192 * odd_row)


def backward_slabs(count, offs, grads, win, incident, ext, right, left):
    slabs = win.shape[0]
    back = (left, right)
    for k in reversed(range(slabs)):
        if grads[0] == "exit":
            fields = grads[1]
        else:
            fields = apply_both(grads[1], back[0], back[1])
        nxt = []
        for p in range(count):
            row, block, shift = place(offs, p)
            piece = conj_times(incident(k, p), fields[p])
            add_window(ext, 0, k, row, block, shift, piece[0])
            add_window(ext, 1, k, row, block, shift, piece[1])
            nxt.append(conj_times(pair(win.at[k], p), fields[p]))
        grads = ("inner", nxt)
    return grads[1]


def middle_kernel(
    count, pos, offs, shifts, wave, win, measured, mats, exits,
    grad, error, center, first, second, strip_l, strip_r, psi, ext,
):
    slabs = win.shape[0]

    @pl.when(pos[0] == 1)
    def _():
        right = (mats[0, 0], mats[0, 1])
        left = (mats[1, 0], mats[1, 1])
        exit_right = (exits[0, 0], exits[0, 1])
        exit_left = (exits[1, 0], exits[1, 1])
        ext[...] = jnp.zeros_like(ext)
        fields = [pair(wave, p) for p in range(count)]
        for k in range(slabs):
            if k:
                for p in range(count):
                    psi[k - 1, p, 0], psi[k - 1, p, 1] = fields[p]
            entering = [times(fields[p], pair(win.at[k], p)) for p in range(count)]
            if k < slabs - 1:
                fields = apply_both(entering, right, left)
            else:
                fields = apply_both(entering, exit_right, exit_left)
        total = jnp.zeros((8, 128), F32)
        far = []
        for p in range(count):
            target = pltpu.roll(measured[p], (128 - shifts[p, 0]) & 127, axis=0)
            target = pltpu.roll(target, (128 - shifts[p, 1]) & 127, axis=1)
            re, im = fields[p]
            residual = re * re + im * im - target
            total = total + jnp.sum((residual * residual).reshape(16, 8, 128), axis=0)
            twice = 2.0 * residual
            far.append((twice * re, twice * im))
        error[...] = total * 0.5
        entry = apply_both(far, exit_left, exit_right)

        def incident(k, p):
            return pair(wave, p) if k == 0 else pair(psi.at[k - 1], p)

        out = backward_slabs(count, offs, ("exit", entry), win, incident, ext, right, left)
        for p in range(count):
            grad[p, 0], grad[p, 1] = out[p]
        emit_gradient(pos, ext, center, first, second, strip_l, strip_r)


def backward_kernel(
    count, pos, offs, grad, win, psi, probe, mats, center1, first1, second1, strip_l1, strip_r1,
    probe_part, center, first, second, strip_l, strip_r, ext,
):
    @pl.when(pos[0] == 1)
    def _():
        center[...] = center1[...]
        first[...] = first1[...]
        second[...] = second1[...]
        strip_l[...] = strip_l1[...]
        strip_r[...] = strip_r1[...]
        probe_part[...] = jnp.zeros_like(probe_part)

    @pl.when(pos[0] == 0)
    def _():
        right = (mats[0, 0], mats[0, 1])
        left = (mats[1, 0], mats[1, 1])
        ext[...] = jnp.zeros_like(ext)

        def incident(k, p):
            return (probe[0], probe[1]) if k == 0 else pair(psi.at[k - 1], p)

        grads = ("inner", [pair(grad, p) for p in range(count)])
        out = backward_slabs(count, offs, grads, win, incident, ext, right, left)
        probe_part[0] = sum(o[0] for o in out[1:]) + out[0][0]
        probe_part[1] = sum(o[1] for o in out[1:]) + out[0][1]
        emit_gradient(pos, ext, center, first, second, strip_l, strip_r)


def fold_rows_kernel(pos, strip_l, strip_r, row1, row2, first, second):
    even = pos[1] == 0

    def put(out, strip, lanes):
        out[...] = strip[...]
        low = pos[2] * 64
        for ref, start in ((row1, 64 - low), (row2, low)):
            rows = pl.ds(pl.multiple_of(start, 64), 64)
            out[:, rows, :] = out[:, rows, :] + ref[:, :, lanes]

    @pl.when(even)
    def _():
        put(first, strip_r, slice(640, 768))
        put(second, strip_l, slice(512, 640))

    @pl.when(jnp.logical_not(even))
    def _():
        put(first, strip_l, slice(512, 640))
        put(second, strip_r, slice(640, 768))


def fold_kernel(pos, center, row1, row2, col1, col2, out):
    even = pos[1] == 0
    out[...] = center[...]
    low = pos[2] * 64
    for ref, start in ((row1, 64 - low), (row2, low)):
        rows = pl.ds(pl.multiple_of(start, 64), 64)
        out[0, :, rows, :] = out[0, :, rows, :] + ref[:, :, 0:256]
        out[1, :, rows, :] = out[1, :, rows, :] + ref[:, :, 256:512]

    def columns(from_left, from_right):
        zero = jnp.zeros(from_left.shape, F32)
        out[0, :, :, :128] = out[0, :, :, :128] + join(from_left[...], zero)
        out[1, :, :, :128] = out[1, :, :, :128] + join(roll_half(from_left[...]), zero)
        out[0, :, :, 128:] = out[0, :, :, 128:] + join(zero, roll_half(from_right[...]))
        out[1, :, :, 128:] = out[1, :, :, 128:] + join(zero, from_right[...])

    @pl.when(even)
    def _():
        columns(col2, col1)

    @pl.when(jnp.logical_not(even))
    def _():
        columns(col1, col2)


def call(kernel, outs, scalars, arrays, scratch=(), flops=0, name=None):
    outs = [jax.ShapeDtypeStruct(s, F32) for s in outs]
    moved = sum(int(np.prod(a.shape)) * 4 for a in list(arrays) + outs)
    return pl.pallas_call(
        kernel,
        out_shape=outs,
        in_specs=[pl.BlockSpec(memory_space=pltpu.SMEM)] * len(scalars)
        + [pl.BlockSpec(memory_space=pltpu.VMEM)] * len(arrays),
        out_specs=[pl.BlockSpec(memory_space=pltpu.VMEM)] * len(outs),
        scratch_shapes=[pltpu.VMEM(s, F32) for s in scratch],
        compiler_params=pltpu.CompilerParams(vmem_limit_bytes=VMEM_LIMIT),
        cost_estimate=pl.CostEstimate(flops=flops, bytes_accessed=moved, transcendentals=0),
        name=name,
    )(*scalars, *arrays)


def swap_even(value, axis):
    size = lax.axis_size(axis)
    return lax.ppermute(value, axis, [(i, i ^ 1) for i in range(size)])


def swap_odd(value, axis):
    size = lax.axis_size(axis)
    return lax.ppermute(value, axis, [(i, ((i - 1) ^ 1) + 1) for i in range(1, size - 1)])


def total_over(value, shape):
    rows, cols, depth = shape
    inner = 4

    def step(move):
        return [((a * cols + b) * depth + d, move(a, b, d)) for a in range(rows) for b in range(cols) for d in range(depth)]

    def flat(a, b, d):
        return (a * cols + b) * depth + d

    axes = ("sx", "sy", "depth")
    moves = []
    moves.append([lambda a, b, d, o=o: flat(a, b // inner * inner + (b % inner + o) % inner, d) for o in range(1, inner)])
    outer = cols // inner
    moves.append([lambda a, b, d, o=o: flat(a, (b // inner + o) % outer * inner + b % inner, d) for o in range(1, outer)])
    for group in moves:
        value = ordered_sum(value, [lax.ppermute(value, axes, step(m)) for m in group])
    for bit in (1, 2):
        value = value + lax.ppermute(value, "sx", [(i, i ^ bit) for i in range(rows)])
    return value


def ordered_sum(value, others):
    return value + others[0] + others[1] + others[2]


def local(probe_wave, transmission, scan_offsets, pattern_shifts, patterns):
    slabs, rows, cols = transmission.shape[1:]
    offs = scan_offsets.reshape(-1, 2)
    shifts = pattern_shifts.reshape(-1, 2)
    count = offs.shape[0]
    measured = patterns.reshape(count, WIN, WIN)
    steps, exits = constants()
    depth = lax.axis_index("depth")
    pos = jnp.stack([depth, lax.axis_index("sy") % 2, lax.axis_index("sx") % 2]).astype(jnp.int32)

    strip = (slabs, rows, 128)
    rim = (slabs, HALF, 768)
    field = (count, 2, WIN, WIN)
    ext = (2, slabs, rows + 2 * HALF + 8, 512)
    step_flops = 2 * 3 * 2 * 256 * 256 * WIN * count

    col1, col2 = call(pack_columns_kernel, [strip, strip], [pos], [transmission], name="pack_columns")
    col1, col2 = swap_even(col1, "sy"), swap_odd(col2, "sy")
    row1, row2 = call(pack_rows_kernel, [rim, rim], [pos], [transmission, col1, col2], name="pack_rows")
    row1, row2 = swap_even(row1, "sx"), swap_odd(row2, "sx")
    wave, win, psi = call(
        functools.partial(forward_kernel, count),
        [field, (slabs,) + field, (slabs - 1,) + field],
        [pos, offs],
        [probe_wave, transmission, col1, col2, row1, row2, steps],
        [ext],
        slabs * step_flops,
        name="forward",
    )
    wave = lax.ppermute(wave, "depth", [(0, 1)])
    grad_outs = [(2, slabs, rows, cols), rim, rim, strip, strip]
    grad, error, *folded = call(
        functools.partial(middle_kernel, count),
        [field, (8, 128)] + grad_outs,
        [pos, offs, shifts],
        [wave, win, measured, steps, exits],
        [(slabs - 1,) + field, ext],
        2 * slabs * step_flops,
        name="middle",
    )
    grad = lax.ppermute(grad, "depth", [(1, 0)])
    probe_part, center, row1, row2, strip_l, strip_r = call(
        functools.partial(backward_kernel, count),
        [(2, WIN, WIN)] + grad_outs,
        [pos, offs],
        [grad, win, psi, probe_wave, steps] + folded,
        [ext],
        slabs * step_flops,
        name="backward",
    )
    row1, row2 = swap_even(row1, "sx"), swap_odd(row2, "sx")
    packet = jnp.concatenate([probe_part.reshape(2 * WIN, WIN), jnp.where(depth == 1, error, 0.0)], axis=0)
    packet = packet + lax.ppermute(packet, "depth", [(0, 1), (1, 0)])
    sizes = (lax.axis_size("sx"), lax.axis_size("sy"), lax.axis_size("depth"))
    packet = total_over(packet, sizes)
    col1, col2 = call(fold_rows_kernel, [strip, strip], [pos], [strip_l, strip_r, row1, row2], name="fold_rows")
    col1, col2 = swap_even(col1, "sy"), swap_odd(col2, "sy")
    (out,) = call(fold_kernel, [(2, slabs, rows, cols)], [pos], [center, row1, row2, col1, col2], name="fold")
    positions = count * sizes[0] * sizes[1]
    probe_grad = packet[: 2 * WIN].reshape(2, WIN, WIN) / positions
    mean_error = jnp.sum(packet[2 * WIN :]) / (positions * WIN * WIN)
    return out, probe_grad, mean_error


def solution(mesh):
    in_specs = (
        P(),
        P(None, "depth", "sx", "sy"),
        P("sx", "sy", None, None),
        P("sx", "sy", None, None),
        P("sx", "sy", None, None, None),
    )
    out_specs = (P(None, "depth", "sx", "sy"), P(), P())
    return jax.shard_map(local, mesh=mesh, in_specs=in_specs, out_specs=out_specs, check_vma=False)
```

```python
import functools

import jax
import jax.numpy as jnp
import numpy as np
from jax import lax
from jax.experimental import pallas as pl
from jax.experimental.pallas import tpu as pltpu
from jax.sharding import PartitionSpec as P


FRESNEL = 12.0
WIN = 128
HALF = 64
TALL = WIN + 8
F32 = jnp.float32
BF16 = jnp.bfloat16
VMEM_LIMIT = 16 * 1024 * 1024


def tables():
    n = np.arange(WIN)
    fourier = np.exp(-2j * np.pi * (np.outer(n, n) % WIN) / WIN) / np.sqrt(WIN)
    freq = np.where(n < WIN // 2, n, n - WIN) / WIN
    phase = np.exp(-1j * FRESNEL * freq * freq)
    prop = fourier.conj() @ (phase[:, None] * fourier)
    exit_left = fourier @ prop
    exit_right = prop @ fourier
    return prop, exit_left, exit_right


def right_block(m):
    return np.block([[m.real, m.imag], [-m.imag, m.real]])


def left_block(m):
    return np.block([[m.real, -m.imag], [m.imag, m.real]])


def halves(m):
    m = m.astype(np.float32)
    hi = m.astype(jnp.bfloat16)
    lo = (m - hi.astype(np.float32)).astype(jnp.bfloat16)
    return np.stack([hi, lo])


def constants():
    prop, exit_left, exit_right = tables()
    steps = np.stack([halves(right_block(prop)), halves(left_block(prop))])
    exits = np.stack([halves(right_block(exit_right)), halves(left_block(exit_left))])
    return jnp.asarray(steps), jnp.asarray(exits)


def split(x):
    hi = x.astype(BF16)
    return hi, (x - hi.astype(F32)).astype(BF16)


def mm(a, b):
    return jnp.dot(a, b, preferred_element_type=F32)


def mm3(a, b):
    return mm(a[0], b[0]) + (mm(a[1], b[0]) + mm(a[0], b[1]))


def apply_both(fields, right, left):
    rows = jnp.concatenate([jnp.concatenate([re, im], axis=1) for re, im in fields], axis=0)
    z = mm3(split(rows), right)
    cols = jnp.concatenate(
        [
            jnp.concatenate([z[p * WIN : (p + 1) * WIN, :WIN], z[p * WIN : (p + 1) * WIN, WIN:]], axis=0)
            for p in range(len(fields))
        ],
        axis=1,
    )
    y = mm3(left, split(cols))
    return [
        (y[:WIN, p * WIN : (p + 1) * WIN], y[WIN:, p * WIN : (p + 1) * WIN]) for p in range(len(fields))
    ]


def times(a, b):
    return a[0] * b[0] - a[1] * b[1], a[0] * b[1] + a[1] * b[0]


def conj_times(a, b):
    return a[0] * b[0] + a[1] * b[1], a[0] * b[1] - a[1] * b[0]


def pair(ref, i):
    return ref[i, 0], ref[i, 1]


def roll_half(x):
    return pltpu.roll(x, HALF, axis=x.ndim - 1)


def join(low, high):
    lane = lax.broadcasted_iota(jnp.int32, low.shape, low.ndim - 1)
    return jnp.where(lane < HALF, low, high)


def fetch(src, dst, sem):
    copy = pltpu.make_async_copy(src, dst, sem)
    copy.start()
    return copy


def pack_kernel(pos, source, col1, col2, row1, row2, tile, sems):
    fetch(source, tile, sems.at[0]).wait()
    right = join(roll_half(tile[0, :, :, 128:]), tile[1, :, :, 128:])
    left = join(tile[0, :, :, :128], roll_half(tile[1, :, :, :128]))
    even = pos[1] == 0

    @pl.when(even)
    def _():
        col1[...] = right
        col2[...] = left

    @pl.when(jnp.logical_not(even))
    def _():
        col1[...] = left
        col2[...] = right

    low = pos[2] * 64
    row1[...] = tile[:, :, pl.ds(pl.multiple_of(64 - low, 64), 64), :]
    row2[...] = tile[:, :, pl.ds(pl.multiple_of(low, 64), 64), :]


def pack_corners_kernel(pos, col1, col2, first, second):
    even = pos[1] == 0
    low = pos[2] * 64
    for out, start in ((first, 64 - low), (second, low)):
        rows = pl.ds(pl.multiple_of(start, 64), 64)

        @pl.when(even)
        def _():
            out[:, :, :128] = col2[:, rows, :]
            out[:, :, 128:] = col1[:, rows, :]

        @pl.when(jnp.logical_not(even))
        def _():
            out[:, :, :128] = col1[:, rows, :]
            out[:, :, 128:] = col2[:, rows, :]


def load_window(ext, c, k, row, block, shift):
    base = pl.multiple_of(row // 8 * 8, 8)
    wide = ext[c, k, pl.ds(base, TALL), pl.ds(pl.multiple_of(block * 128, 128), 256)]
    wide = pltpu.roll(wide, (256 - shift) & 255, axis=1)[:, :WIN]
    return pltpu.roll(wide, (TALL - row % 8) % TALL, axis=0)[:WIN]


def place(pos, p):
    row = pos[3 + 2 * p] + HALF
    col = pos[4 + 2 * p] + 128
    return row, col // 128, col % 128


def forward_kernel(
    count, pos, probe_h, tile, col1_h, col2_h, row1, row2, crn1_h, crn2_h, mats_h,
    wave, win, psi_h, ext, probe, mats, psi, cols, corners, sems,
):
    slabs = tile.shape[1]
    odd_row = pos[2]
    starts = (pl.multiple_of(192 * (1 - odd_row), 64), pl.multiple_of(192 * odd_row, 64))
    first = pos[1]
    near = [
        fetch(col1_h, cols.at[1 - first], sems.at[0]),
        fetch(col2_h, cols.at[first], sems.at[1]),
        fetch(crn1_h, corners.at[0], sems.at[2]),
        fetch(crn2_h, corners.at[1], sems.at[3]),
    ]
    far = [
        fetch(tile, ext.at[:, :, pl.ds(64, 128), pl.ds(128, 256)], sems.at[4]),
        fetch(row1, ext.at[:, :, pl.ds(starts[0], 64), pl.ds(128, 256)], sems.at[5]),
        fetch(row2, ext.at[:, :, pl.ds(starts[1], 64), pl.ds(128, 256)], sems.at[6]),
    ]
    loads = [fetch(probe_h, probe, sems.at[7]), fetch(mats_h, mats, sems.at[8])]
    for copy in near:
        copy.wait()

    def sides(rows, left, right):
        ext[0, :, rows, 0:128] = roll_half(left)
        ext[1, :, rows, 0:128] = left
        ext[0, :, rows, 384:512] = right
        ext[1, :, rows, 384:512] = roll_half(right)

    sides(slice(64, 192), cols[0], cols[1])
    for i in range(2):
        sides(pl.ds(starts[i], 64), corners[i, :, :, :128], corners[i, :, :, 128:])
    for copy in far:
        copy.wait()
    for copy in loads:
        copy.wait()
    for p in range(count):
        row, block, shift = place(pos, p)
        for k in range(slabs):
            win[k, p, 0] = load_window(ext, 0, k, row, block, shift) + 1.0
            win[k, p, 1] = load_window(ext, 1, k, row, block, shift)

    @pl.when(pos[0] == 0)
    def _():
        right = (mats[0, 0], mats[0, 1])
        left = (mats[1, 0], mats[1, 1])
        fields = [(probe[0], probe[1])] * count
        saves = []
        for k in range(slabs):
            if k:
                for p in range(count):
                    psi[k - 1, p, 0], psi[k - 1, p, 1] = fields[p]
                saves.append(fetch(psi.at[k - 1], psi_h.at[k - 1], sems.at[8 + k]))
            fields = apply_both([times(fields[p], pair(win.at[k], p)) for p in range(count)], right, left)
        for p in range(count):
            wave[p, 0], wave[p, 1] = fields[p]
        for copy in saves:
            copy.wait()


def add_window(ext, c, k, row, block, shift, piece):
    tall = pltpu.roll(jnp.concatenate([piece, jnp.zeros((TALL - WIN, WIN), F32)], axis=0), row % 8, axis=0)
    wide = pltpu.roll(jnp.concatenate([tall, jnp.zeros_like(tall)], axis=1), shift, axis=1)
    base = pl.multiple_of(row // 8 * 8, 8)
    at = (c, k, pl.ds(base, TALL), pl.ds(pl.multiple_of(block * 128, 128), 256))
    ext[at] = ext[at] + wide


def strips(ext, rows):
    left = join(roll_half(ext[0, :, rows, 0:128]), ext[1, :, rows, 0:128])
    right = join(ext[0, :, rows, 384:512], roll_half(ext[1, :, rows, 384:512]))
    return left, right


def emit_rims(pos, ext, first, second):
    def rim(out, start):
        rows = pl.ds(pl.multiple_of(start, 64), 64)
        out[:, :, 0:256] = ext[0, :, rows, 128:384]
        out[:, :, 256:512] = ext[1, :, rows, 128:384]
        out[:, :, 512:640], out[:, :, 640:768] = strips(ext, rows)

    odd_row = pos[2]
    rim(first, 192 * (1 - odd_row))
    rim(second, 192 * odd_row)


def backward_slabs(count, pos, grads, win, incident, ext, right, left, ext_h, sems):
    slabs = win.shape[0]
    saves = []
    for k in reversed(range(slabs)):
        if grads[0] == "exit":
            fields = grads[1]
        else:
            fields = apply_both(grads[1], left, right)
        nxt = []
        for p in range(count):
            row, block, shift = place(pos, p)
            piece = conj_times(incident(k, p), fields[p])
            add_window(ext, 0, k, row, block, shift, piece[0])
            add_window(ext, 1, k, row, block, shift, piece[1])
            nxt.append(conj_times(pair(win.at[k], p), fields[p]))
        saves.append(fetch(ext.at[:, k], ext_h.at[:, k], sems.at[k]))
        grads = ("inner", nxt)
    return grads[1], saves


def middle_kernel(
    count, pos, wave, win, measured_h, mats_h, exits_h, grad, error, ext_h, ext, psi, measured, mats, exits, sems
):
    slabs = win.shape[0]

    @pl.when(pos[0] == 0)
    def _():
        error[...] = jnp.zeros_like(error)

    @pl.when(pos[0] == 1)
    def _():
        loads = [
            fetch(mats_h, mats, sems.at[slabs]),
            fetch(exits_h, exits, sems.at[slabs + 1]),
            fetch(measured_h, measured, sems.at[slabs + 2]),
        ]
        ext[...] = jnp.zeros_like(ext)
        for copy in loads:
            copy.wait()
        right = (mats[0, 0], mats[0, 1])
        left = (mats[1, 0], mats[1, 1])
        exit_right = (exits[0, 0], exits[0, 1])
        exit_left = (exits[1, 0], exits[1, 1])
        fields = [pair(wave, p) for p in range(count)]
        for k in range(slabs):
            if k:
                for p in range(count):
                    psi[k - 1, p, 0], psi[k - 1, p, 1] = fields[p]
            entering = [times(fields[p], pair(win.at[k], p)) for p in range(count)]
            if k < slabs - 1:
                fields = apply_both(entering, right, left)
            else:
                fields = apply_both(entering, exit_right, exit_left)
        total = jnp.zeros((8, 128), F32)
        far = []
        for p in range(count):
            at = 3 + 2 * count + 2 * p
            target = pltpu.roll(measured[p], (128 - pos[at]) & 127, axis=0)
            target = pltpu.roll(target, (128 - pos[at + 1]) & 127, axis=1)
            re, im = fields[p]
            residual = re * re + im * im - target
            total = total + jnp.sum((residual * residual).reshape(16, 8, 128), axis=0)
            twice = 2.0 * residual
            far.append((twice * re, twice * im))
        error[...] = jnp.full((8, 128), 0.5 * jnp.sum(total), F32)
        entry = apply_both(far, exit_left, exit_right)

        def incident(k, p):
            return pair(wave, p) if k == 0 else pair(psi.at[k - 1], p)

        out, saves = backward_slabs(count, pos, ("exit", entry), win, incident, ext, right, left, ext_h, sems)
        for p in range(count):
            grad[p, 0], grad[p, 1] = out[p]
        for copy in saves:
            copy.wait()


def backward_kernel(
    count, pos, grad, win, psi_h, probe_h, mats_h, ext1_h, error,
    keep, send, ext_h, first, second, ext, probe, mats, psi, sems,
):
    slabs = win.shape[0]

    def packet(re, im):
        upper = jnp.concatenate([im[8:], error[...]], axis=0)
        lower = jnp.concatenate([re, im[:8]], axis=0)

        @pl.when(pos[2] == 0)
        def _():
            keep[...] = lower
            send[0:128, :] = upper
            send[128:136, :] = jnp.zeros((8, 128), F32)

        @pl.when(pos[2] == 1)
        def _():
            keep[0:128, :] = upper
            keep[128:136, :] = jnp.zeros((8, 128), F32)
            send[...] = lower

    @pl.when(pos[0] == 1)
    def _():
        load = fetch(ext1_h, ext, sems.at[0])
        zero = jnp.zeros((WIN, WIN), F32)
        packet(zero, zero)
        load.wait()
        emit_rims(pos, ext, first, second)

    @pl.when(pos[0] == 0)
    def _():
        loads = [
            fetch(mats_h, mats, sems.at[slabs]),
            fetch(psi_h, psi, sems.at[slabs + 1]),
            fetch(probe_h, probe, sems.at[slabs + 2]),
        ]
        ext[...] = jnp.zeros_like(ext)
        for copy in loads:
            copy.wait()
        right = (mats[0, 0], mats[0, 1])
        left = (mats[1, 0], mats[1, 1])

        def incident(k, p):
            return (probe[0], probe[1]) if k == 0 else pair(psi.at[k - 1], p)

        grads = ("inner", [pair(grad, p) for p in range(count)])
        out, saves = backward_slabs(count, pos, grads, win, incident, ext, right, left, ext_h, sems)
        packet(sum(o[0] for o in out[1:]) + out[0][0], sum(o[1] for o in out[1:]) + out[0][1])
        emit_rims(pos, ext, first, second)
        for copy in saves:
            copy.wait()


def fold_rows_kernel(pos, ext_h, row1, row2, first, second, outer, sems):
    loads = [
        fetch(ext_h.at[:, :, pl.ds(64, 128), pl.ds(0, 128)], outer.at[0], sems.at[0]),
        fetch(ext_h.at[:, :, pl.ds(64, 128), pl.ds(384, 128)], outer.at[1], sems.at[1]),
    ]
    for copy in loads:
        copy.wait()
    even = pos[1] == 0
    low = pos[2] * 64
    strip_l = join(roll_half(outer[0, 0]), outer[0, 1])
    strip_r = join(outer[1, 0], roll_half(outer[1, 1]))

    def put(out, strip, lanes):
        out[...] = strip
        for ref, start in ((row1, 64 - low), (row2, low)):
            rows = pl.ds(pl.multiple_of(start, 64), 64)
            out[:, rows, :] = out[:, rows, :] + ref[:, :, lanes]

    @pl.when(even)
    def _():
        put(first, strip_r, slice(640, 768))
        put(second, strip_l, slice(512, 640))

    @pl.when(jnp.logical_not(even))
    def _():
        put(first, strip_l, slice(512, 640))
        put(second, strip_r, slice(640, 768))


def fold_kernel(pos, ext_h, row1, row2, col1, col2, out, sems):
    fetch(ext_h.at[:, :, pl.ds(64, 128), pl.ds(128, 256)], out, sems.at[0]).wait()
    even = pos[1] == 0
    low = pos[2] * 64
    for ref, start in ((row1, 64 - low), (row2, low)):
        rows = pl.ds(pl.multiple_of(start, 64), 64)
        out[0, :, rows, :] = out[0, :, rows, :] + ref[:, :, 0:256]
        out[1, :, rows, :] = out[1, :, rows, :] + ref[:, :, 256:512]

    def columns(from_left, from_right):
        zero = jnp.zeros(from_left.shape, F32)
        out[0, :, :, :128] = out[0, :, :, :128] + join(from_left[...], zero)
        out[1, :, :, :128] = out[1, :, :, :128] + join(roll_half(from_left[...]), zero)
        out[0, :, :, 128:] = out[0, :, :, 128:] + join(zero, roll_half(from_right[...]))
        out[1, :, :, 128:] = out[1, :, :, 128:] + join(zero, from_right[...])

    @pl.when(even)
    def _():
        columns(col2, col1)

    @pl.when(jnp.logical_not(even))
    def _():
        columns(col1, col2)


def finish_kernel(scales, pos, keep, back, probe, error):
    def put(lower, upper):
        probe[0] = lower[0:128, :] * scales[0]
        probe[1, 0:8, :] = lower[128:136, :] * scales[0]
        probe[1, 8:128, :] = upper[0:120, :] * scales[0]
        error[0, 0] = jnp.max(upper[120:128, :]) * scales[1]

    @pl.when(pos[2] == 0)
    def _():
        put(keep, back)

    @pl.when(pos[2] == 1)
    def _():
        put(back, keep)


HBM = pltpu.MemorySpace.HBM
VMEM = pltpu.MemorySpace.VMEM


def call(kernel, outs, scalars, arrays, scratch=(), flops=0, hbm=(), hbm_out=(), smem_out=(), fixed=(), aliases=None):
    outs = [jax.ShapeDtypeStruct(s, F32) for s in outs]
    moved = sum(int(np.prod(a.shape)) * 4 for a in list(arrays) + outs)
    arrays = [pltpu.with_memory_space_constraint(a, HBM) if i in fixed else a for i, a in enumerate(arrays)]
    return pl.pallas_call(
        kernel,
        out_shape=outs,
        in_specs=[pl.BlockSpec(memory_space=pltpu.SMEM)] * len(scalars)
        + [pl.BlockSpec(memory_space=HBM if i in hbm else VMEM) for i in range(len(arrays))],
        out_specs=[
            pl.BlockSpec(memory_space=HBM if i in hbm_out else pltpu.SMEM if i in smem_out else VMEM)
            for i in range(len(outs))
        ],
        scratch_shapes=list(scratch),
        input_output_aliases=aliases or {},
        compiler_params=pltpu.CompilerParams(vmem_limit_bytes=VMEM_LIMIT),
        cost_estimate=pl.CostEstimate(flops=flops, bytes_accessed=moved, transcendentals=0),
    )(*scalars, *arrays)


def swap(value, axis, odd=False):
    size = lax.axis_size(axis)
    pairs = [(i, ((i - 1) ^ 1) + 1) for i in range(1, size - 1)] if odd else [(i, i ^ 1) for i in range(size)]
    return lax.ppermute(value, axis, pairs)


AXES = ("sx", "sy", "depth")


def ring_sum(value, sizes, turn):
    rows, cols, depth = sizes

    def flat(a, b, d):
        return (a * cols + b) * depth + d

    got = []
    for step in (1, 2, 3):
        pairs = [
            (flat(a, b, d), flat(*turn(a, b, d, step))) for a in range(rows) for b in range(cols) for d in range(depth)
        ]
        got.append(lax.ppermute(value, AXES, pairs))
    return (value + got[1]) + (got[0] + got[2])


def turn_x(a, b, d, step):
    return a, b // 4 * 4 + (b + step) % 4, d


def turn_z(a, b, d, step):
    return a, (b // 4 + step) % 4 * 4 + b % 4, d


def turn_y(a, b, d, step):
    y = (a // 2 * 2 + d + step) % 4
    return y // 2 * 2 + a % 2, b, y % 2


def local(probe_wave, transmission, scan_offsets, pattern_shifts, patterns):
    slabs, rows, cols = transmission.shape[1:]
    count = scan_offsets.shape[2]
    measured = patterns.reshape(count, WIN, WIN)
    steps, exits = constants()
    core = lax.axis_index("sx") % 2
    where = jnp.stack([lax.axis_index("depth"), lax.axis_index("sy") % 2, core]).astype(jnp.int32)
    pos = jnp.concatenate([where, scan_offsets.reshape(-1), pattern_shifts.reshape(-1)])
    sizes = (lax.axis_size("sx"), lax.axis_size("sy"), lax.axis_size("depth"))

    tile = (2, slabs, rows, cols)
    strip = (slabs, rows, 128)
    rim = (slabs, HALF, 768)
    side = (2, slabs, HALF, cols)
    corner = (slabs, HALF, 256)
    field = (count, 2, WIN, WIN)
    inner = (slabs - 1,) + field
    ext = (2, slabs, rows + 2 * HALF + 8, 512)
    step_flops = 2 * 3 * 2 * 256 * 256 * WIN * count

    def vmem(shape, dtype=F32):
        return pltpu.VMEM(shape, dtype)

    def sems(n):
        return pltpu.SemaphoreType.DMA((n,))

    mats = vmem(steps.shape, BF16)
    probe = vmem(probe_wave.shape)

    col1, col2, row1, row2 = call(
        pack_kernel, [strip, strip, side, side], [where], [transmission], [vmem(tile), sems(1)], hbm=(0,), fixed=(0,)
    )
    col1, col2 = swap(col1, "sy"), swap(col2, "sy", True)
    row1, row2 = swap(row1, "sx"), swap(row2, "sx", True)
    crn1, crn2 = call(pack_corners_kernel, [corner, corner], [where], [col1, col2])
    crn1, crn2 = swap(crn1, "sx"), swap(crn2, "sx", True)
    wave, win, psi = call(
        functools.partial(forward_kernel, count),
        [field, (slabs,) + field, inner],
        [pos],
        [probe_wave, transmission, col1, col2, row1, row2, crn1, crn2, steps],
        [vmem(ext), probe, mats, vmem(inner), vmem((2,) + strip), vmem((2,) + corner), sems(slabs + 8)],
        slabs * step_flops,
        hbm=tuple(range(9)),
        fixed=(0, 1, 8),
        hbm_out=(2,),
    )
    wave = lax.ppermute(wave, "depth", [(0, 1)])
    grad, error, edge = call(
        functools.partial(middle_kernel, count),
        [field, (8, 128), ext],
        [pos],
        [wave, win, measured, steps, exits],
        [vmem(ext), vmem(inner), vmem(measured.shape), mats, mats, sems(slabs + 3)],
        2 * slabs * step_flops,
        hbm=(2, 3, 4),
        fixed=(2, 3, 4),
        hbm_out=(2,),
    )
    grad = lax.ppermute(grad, "depth", [(1, 0)])
    part, other, edge, row1, row2 = call(
        functools.partial(backward_kernel, count),
        [(136, WIN), (136, WIN), ext, rim, rim],
        [pos],
        [grad, win, psi, probe_wave, steps, edge, error],
        [vmem(ext), probe, mats, vmem(inner), sems(slabs + 3)],
        slabs * step_flops,
        hbm=(2, 3, 4, 5),
        fixed=(3, 4),
        hbm_out=(2,),
        aliases={6: 2},
    )
    row1, row2 = swap(row1, "sx"), swap(row2, "sx", True)
    part = part + swap(other, "sx")
    part = ring_sum(part, sizes, turn_x)
    part, row1, row2 = lax.optimization_barrier((part, row1, row2))
    col1, col2 = call(
        fold_rows_kernel, [strip, strip], [where], [edge, row1, row2],
        [vmem((2, 2) + strip), sems(2)], hbm=(0,),
    )
    part, col1, col2 = lax.optimization_barrier((part, col1, col2))
    col1, col2 = swap(col1, "sy"), swap(col2, "sy", True)
    part = ring_sum(part, sizes, turn_z)
    part, col1, col2 = lax.optimization_barrier((part, col1, col2))
    (out,) = call(fold_kernel, [tile], [where], [edge, row1, row2, col1, col2], [sems(1)], hbm=(0,))
    part = ring_sum(part, sizes, turn_y)
    other = swap(part, "sx")
    positions = count * sizes[0] * sizes[1]
    scales = jnp.array([1.0 / positions, 1.0 / (positions * WIN * WIN)], F32)
    probe_grad, error = call(finish_kernel, [(2, WIN, WIN), (1, 1)], [scales, where], [part, other], smem_out=(1,))
    return out, probe_grad, error.reshape(())


def solution(mesh):
    in_specs = (
        P(),
        P(None, "depth", "sx", "sy"),
        P("sx", "sy", None, None),
        P("sx", "sy", None, None),
        P("sx", "sy", None, None, None),
    )
    out_specs = (P(None, "depth", "sx", "sy"), P(), P())
    return jax.shard_map(local, mesh=mesh, in_specs=in_specs, out_specs=out_specs, check_vma=False)
```

```python
import functools

import jax
import jax.numpy as jnp
import numpy as np
from jax import lax
from jax.experimental import pallas as pl
from jax.experimental.pallas import tpu as pltpu
from jax.sharding import PartitionSpec as P


FRESNEL = 12.0
WIN = 128
HALF = 64
TALL = WIN + 8
LEAD = 4
F32 = jnp.float32
BF16 = jnp.bfloat16
VMEM_LIMIT = 16 * 1024 * 1024


def tables():
    n = np.arange(WIN)
    fourier = np.exp(-2j * np.pi * (np.outer(n, n) % WIN) / WIN) / np.sqrt(WIN)
    freq = np.where(n < WIN // 2, n, n - WIN) / WIN
    phase = np.exp(-1j * FRESNEL * freq * freq)
    prop = fourier.conj() @ (phase[:, None] * fourier)
    exit_left = fourier @ prop
    exit_right = prop @ fourier
    return prop, exit_left, exit_right


def right_block(m):
    return np.block([[m.real, m.imag], [-m.imag, m.real]])


def left_block(m):
    return np.block([[m.real, -m.imag], [m.imag, m.real]])


def halves(m):
    m = m.astype(np.float32)
    hi = m.astype(jnp.bfloat16)
    lo = (m - hi.astype(np.float32)).astype(jnp.bfloat16)
    return np.stack([hi, lo])


def constants():
    prop, exit_left, exit_right = tables()
    steps = halves(right_block(prop))
    exits = np.stack([halves(right_block(exit_right)), halves(left_block(exit_left))])
    return jnp.asarray(steps), jnp.asarray(exits)


def step_pair(mats):
    right = (mats[0], mats[1])

    def other(m):
        top = jnp.concatenate([m[:WIN, :WIN], m[WIN:, :WIN]], axis=1)
        bottom = jnp.concatenate([m[:WIN, WIN:], m[WIN:, WIN:]], axis=1)
        return jnp.concatenate([top, bottom], axis=0)

    return right, (other(right[0]), other(right[1]))


def split(x):
    hi = x.astype(BF16)
    return hi, (x - hi.astype(F32)).astype(BF16)


def mm(a, b):
    return jnp.dot(a, b, preferred_element_type=F32)


def mm3(a, b):
    return mm(jnp.concatenate([a[0], a[1], a[0]], axis=1), jnp.concatenate([b[0], b[0], b[1]], axis=0))


def apply_both(fields, right, left):
    rows = jnp.concatenate([jnp.concatenate([re, im], axis=1) for re, im in fields], axis=0)
    z = mm3(split(rows), right)
    cols = jnp.concatenate(
        [
            jnp.concatenate([z[p * WIN : (p + 1) * WIN, :WIN], z[p * WIN : (p + 1) * WIN, WIN:]], axis=0)
            for p in range(len(fields))
        ],
        axis=1,
    )
    y = mm3(left, split(cols))
    return [
        (y[:WIN, p * WIN : (p + 1) * WIN], y[WIN:, p * WIN : (p + 1) * WIN]) for p in range(len(fields))
    ]


def times(a, b):
    return a[0] * b[0] - a[1] * b[1], a[0] * b[1] + a[1] * b[0]


def conj_times(a, b):
    return a[0] * b[0] + a[1] * b[1], a[0] * b[1] - a[1] * b[0]


def pair(ref, i):
    return ref[i, 0], ref[i, 1]


def roll_half(x):
    return pltpu.roll(x, HALF, axis=x.ndim - 1)


def join(low, high):
    lane = lax.broadcasted_iota(jnp.int32, low.shape, low.ndim - 1)
    return jnp.where(lane < HALF, low, high)


def fetch(src, dst, sem):
    copy = pltpu.make_async_copy(src, dst, sem)
    copy.start()
    return copy


def pack_kernel(pos, source, col1, col2, row1, row2, tile, sems):
    fetch(source, tile, sems.at[0]).wait()
    right = join(roll_half(tile[0, :, :, 128:]), tile[1, :, :, 128:])
    left = join(tile[0, :, :, :128], roll_half(tile[1, :, :, :128]))
    even = pos[1] == 0

    @pl.when(even)
    def _():
        col1[...] = right
        col2[...] = left

    @pl.when(jnp.logical_not(even))
    def _():
        col1[...] = left
        col2[...] = right

    low = pos[2] * 64
    row1[...] = tile[:, :, pl.ds(pl.multiple_of(64 - low, 64), 64), :]
    row2[...] = tile[:, :, pl.ds(pl.multiple_of(low, 64), 64), :]


def pack_corners_kernel(pos, col1, col2, first, second):
    even = pos[1] == 0
    low = pos[2] * 64
    for out, start in ((first, 64 - low), (second, low)):
        rows = pl.ds(pl.multiple_of(start, 64), 64)
        ring = inside(pos, col2[:, rows, :])

        @pl.when(even)
        def _():
            out[:, :, :128] = ring
            out[:, :, 128:] = col1[:, rows, :]

        @pl.when(jnp.logical_not(even))
        def _():
            out[:, :, :128] = col1[:, rows, :]
            out[:, :, 128:] = ring


def inside(pos, value):
    return jnp.where(pos[3] == 1, 0.0, value)


def load_window(ext, c, k, row, block, shift):
    base = pl.multiple_of(row // 8 * 8, 8)
    wide = ext[c, k, pl.ds(base, TALL), pl.ds(pl.multiple_of(block * 128, 128), 256)]
    wide = pltpu.roll(wide, (256 - shift) & 255, axis=1)[:, :WIN]
    return pltpu.roll(wide, (TALL - row % 8) % TALL, axis=0)[:WIN]


def place(pos, p):
    row = pos[LEAD + 2 * p] + HALF
    col = pos[LEAD + 1 + 2 * p] + 128
    return row, col // 128, col % 128


def assemble(pos, tile, cols_h, rows_h, corners_h, ext, cols, corners, sems):
    odd_row = pos[2]
    starts = (pl.multiple_of(192 * (1 - odd_row), 64), pl.multiple_of(192 * odd_row, 64))
    first = pos[1]
    near = [
        fetch(cols_h[0], cols.at[1 - first], sems.at[0]),
        fetch(cols_h[1], cols.at[first], sems.at[1]),
        fetch(corners_h[0], corners.at[0], sems.at[2]),
        fetch(corners_h[1], corners.at[1], sems.at[3]),
    ]
    far = [
        fetch(tile, ext.at[:, :, pl.ds(64, 128), pl.ds(128, 256)], sems.at[4]),
        fetch(rows_h[0], ext.at[:, :, pl.ds(starts[0], 64), pl.ds(128, 256)], sems.at[5]),
        fetch(rows_h[1], ext.at[:, :, pl.ds(starts[1], 64), pl.ds(128, 256)], sems.at[6]),
    ]
    for copy in near:
        copy.wait()

    def sides(rows, left, right):
        ext[0, :, rows, 0:128] = roll_half(left)
        ext[1, :, rows, 0:128] = left
        ext[0, :, rows, 384:512] = right
        ext[1, :, rows, 384:512] = roll_half(right)

    cols[first] = inside(pos, cols[first])
    sides(slice(64, 192), cols[0], cols[1])
    for i in range(2):
        sides(pl.ds(starts[i], 64), corners[i, :, :, :128], corners[i, :, :, 128:])
    for copy in far:
        copy.wait()


def cut_window(pos, ext, p, k, win):
    row, block, shift = place(pos, p)
    win[k, p, 0] = load_window(ext, 0, k, row, block, shift) + 1.0
    win[k, p, 1] = load_window(ext, 1, k, row, block, shift)


def run_forward(span, probe, mats, win, wave, psi_h, psi, sems, after):
    slabs = win.shape[0]
    right, left = step_pair(mats)
    fields = [(probe[0], probe[1])] * len(span)
    saves = []
    for k in range(slabs):
        if k:
            for i in range(len(span)):
                psi[k - 1, i, 0], psi[k - 1, i, 1] = fields[i]
            saves.append(fetch(psi.at[k - 1], psi_h.at[k - 1], sems.at[8 + k]))
        fields = apply_both([times(fields[i], pair(win.at[k], p)) for i, p in enumerate(span)], right, left)
        after(k)
    for i in range(len(span)):
        wave[i, 0], wave[i, 1] = fields[i]
    for copy in saves:
        copy.wait()


def forward_first_kernel(
    spans, pos, probe_h, tile, col1_h, col2_h, row1, row2, crn1_h, crn2_h, mats_h,
    wave, win, psi_h, ext, probe, mats, psi, cols, corners, sems,
):
    slabs = tile.shape[1]

    @pl.when(pos[0] == 0)
    def _():
        loads = [fetch(probe_h, probe, sems.at[7]), fetch(mats_h, mats, sems.at[8])]
        assemble(pos, tile, (col1_h, col2_h), (row1, row2), (crn1_h, crn2_h), ext, cols, corners, sems)
        for copy in loads:
            copy.wait()
        for k in range(slabs):
            for p in spans[0]:
                cut_window(pos, ext, p, k, win)

        def after(k):
            for p in spans[1]:
                cut_window(pos, ext, p, k, win)

        run_forward(spans[0], probe, mats, win, wave, psi_h, psi, sems, after)


def forward_second_kernel(spans, pos, probe_h, win, mats_h, wave, psi_h, probe, mats, psi, sems):
    @pl.when(pos[0] == 0)
    def _():
        loads = [fetch(probe_h, probe, sems.at[7]), fetch(mats_h, mats, sems.at[8])]
        for copy in loads:
            copy.wait()
        run_forward(spans[1], probe, mats, win, wave, psi_h, psi, sems, lambda k: None)


def cut_kernel(count, pos, tile, col1_h, col2_h, row1, row2, crn1_h, crn2_h, win, ext, cols, corners, sems):
    slabs = tile.shape[1]

    @pl.when(pos[0] == 1)
    def _():
        assemble(pos, tile, (col1_h, col2_h), (row1, row2), (crn1_h, crn2_h), ext, cols, corners, sems)

        @pl.loop(0, count)
        def _(p):
            for k in range(slabs):
                cut_window(pos, ext, p, k, win)


def add_window(ext, c, k, row, block, shift, piece):
    tall = pltpu.roll(jnp.concatenate([piece, jnp.zeros((TALL - WIN, WIN), F32)], axis=0), row % 8, axis=0)
    wide = pltpu.roll(jnp.concatenate([tall, jnp.zeros_like(tall)], axis=1), shift, axis=1)
    base = pl.multiple_of(row // 8 * 8, 8)
    at = (c, k, pl.ds(base, TALL), pl.ds(pl.multiple_of(block * 128, 128), 256))
    ext[at] = ext[at] + wide


def strips(ext, rows):
    left = join(roll_half(ext[0, :, rows, 0:128]), ext[1, :, rows, 0:128])
    right = join(ext[0, :, rows, 384:512], roll_half(ext[1, :, rows, 384:512]))
    return left, right


def emit_rims(pos, ext, first, second):
    def rim(out, start):
        rows = pl.ds(pl.multiple_of(start, 64), 64)
        out[:, :, 0:256] = ext[0, :, rows, 128:384]
        out[:, :, 256:512] = ext[1, :, rows, 128:384]
        out[:, :, 512:640], out[:, :, 640:768] = strips(ext, rows)

    odd_row = pos[2]
    rim(first, 192 * (1 - odd_row))
    rim(second, 192 * odd_row)


def backward_slabs(span, pos, grads, win, incident, ext, right, left, ext_h, sems, loads):
    slabs = win.shape[0]
    saves = []
    for k in reversed(range(slabs)):
        if grads[0] == "exit":
            fields = grads[1]
        else:
            fields = apply_both(grads[1], left, right)
        if loads:
            loads[k].wait()
        nxt = []
        for i, p in enumerate(span):
            row, block, shift = place(pos, p)
            piece = conj_times(incident(k, i), fields[i])
            add_window(ext, 0, k, row, block, shift, piece[0])
            add_window(ext, 1, k, row, block, shift, piece[1])
            nxt.append(conj_times(pair(win.at[k], p), fields[i]))
        saves.append(fetch(ext.at[:, k], ext_h.at[:, k], sems.at[k]))
        grads = ("inner", nxt)
    return grads[1], saves


def start_ext(group, ext, held_h, sems, at, slabs):
    if group == 0:
        ext[...] = jnp.zeros_like(ext)
        return None
    return [fetch(held_h.at[:, k], ext.at[:, k], sems.at[at + k]) for k in range(slabs)]


def middle_body(
    group, count, span, pos, wave, win, measured_h, mats_h, exits_h, held_h, before,
    grad, error, ext_h, ext, psi, measured, mats, exits, sems,
):
    slabs = win.shape[0]
    extra = slabs + 3

    @pl.when(pos[0] == 0)
    def _():
        error[...] = jnp.zeros_like(error)

    @pl.when(pos[0] == 1)
    def _():
        loads = [
            fetch(mats_h, mats, sems.at[slabs]),
            fetch(exits_h, exits, sems.at[slabs + 1]),
            fetch(measured_h.at[pl.ds(span[0], len(span))], measured, sems.at[slabs + 2]),
        ]
        held = start_ext(group, ext, held_h, sems, extra, slabs)
        for copy in loads:
            copy.wait()
        right, left = step_pair(mats)
        exit_right = (exits[0, 0], exits[0, 1])
        exit_left = (exits[1, 0], exits[1, 1])
        fields = [pair(wave, i) for i in range(len(span))]
        for k in range(slabs):
            if k:
                for i in range(len(span)):
                    psi[k - 1, i, 0], psi[k - 1, i, 1] = fields[i]
            entering = [times(fields[i], pair(win.at[k], p)) for i, p in enumerate(span)]
            if k < slabs - 1:
                fields = apply_both(entering, right, left)
            else:
                fields = apply_both(entering, exit_right, exit_left)
        total = jnp.zeros((8, 128), F32)
        far = []
        for i, p in enumerate(span):
            at = LEAD + 2 * count + 2 * p
            target = pltpu.roll(measured[i], (128 - pos[at]) & 127, axis=0)
            target = pltpu.roll(target, (128 - pos[at + 1]) & 127, axis=1)
            re, im = fields[i]
            residual = re * re + im * im - target
            total = total + jnp.sum((residual * residual).reshape(16, 8, 128), axis=0)
            twice = 2.0 * residual
            far.append((twice * re, twice * im))
        part = jnp.full((8, 128), 0.5 * jnp.sum(total), F32)
        error[...] = part if group == 0 else before[...] + part
        entry = apply_both(far, exit_left, exit_right)

        def incident(k, i):
            return pair(wave, i) if k == 0 else pair(psi.at[k - 1], i)

        out, saves = backward_slabs(span, pos, ("exit", entry), win, incident, ext, right, left, ext_h, sems, held)
        for i in range(len(span)):
            grad[i, 0], grad[i, 1] = out[i]
        for copy in saves:
            copy.wait()


def middle_first_kernel(count, span, pos, wave, win, measured_h, mats_h, exits_h, *rest):
    middle_body(0, count, span, pos, wave, win, measured_h, mats_h, exits_h, None, None, *rest)


def middle_second_kernel(count, span, pos, wave, win, measured_h, mats_h, exits_h, held_h, before, *rest):
    middle_body(1, count, span, pos, wave, win, measured_h, mats_h, exits_h, held_h, before, *rest)


def run_backward(group, span, pos, grad, win, psi_h, probe_h, mats_h, held_h, ext_h, ext, probe, mats, psi, sems):
    slabs = win.shape[0]
    loads = [
        fetch(mats_h, mats, sems.at[slabs]),
        fetch(psi_h, psi, sems.at[slabs + 1]),
        fetch(probe_h, probe, sems.at[slabs + 2]),
    ]
    held = start_ext(group, ext, held_h, sems, slabs + 3, slabs)
    for copy in loads:
        copy.wait()
    right, left = step_pair(mats)

    def incident(k, i):
        return (probe[0], probe[1]) if k == 0 else pair(psi.at[k - 1], i)

    grads = ("inner", [pair(grad, i) for i in range(len(span))])
    out, saves = backward_slabs(span, pos, grads, win, incident, ext, right, left, ext_h, sems, held)
    re = sum(o[0] for o in out[1:]) + out[0][0]
    im = sum(o[1] for o in out[1:]) + out[0][1]
    return re, im, saves


def backward_first_kernel(
    span, pos, grad, win, psi_h, probe_h, mats_h, held_h, total, ext_h, ext, probe, mats, psi, sems
):
    @pl.when(pos[0] == 0)
    def _():
        re, im, saves = run_backward(
            0, span, pos, grad, win, psi_h, probe_h, mats_h, held_h, ext_h, ext, probe, mats, psi, sems
        )
        total[0] = re
        total[1] = im
        for copy in saves:
            copy.wait()


def backward_second_kernel(
    span, pos, grad, win, psi_h, probe_h, mats_h, held_h, error, total,
    keep, send, ext_h, first, second, ext, probe, mats, psi, sems,
):
    def packet(re, im):
        upper = jnp.concatenate([im[8:], error[...]], axis=0)
        lower = jnp.concatenate([re, im[:8]], axis=0)

        @pl.when(pos[2] == 0)
        def _():
            keep[...] = lower
            send[0:128, :] = upper
            send[128:136, :] = jnp.zeros((8, 128), F32)

        @pl.when(pos[2] == 1)
        def _():
            keep[0:128, :] = upper
            keep[128:136, :] = jnp.zeros((8, 128), F32)
            send[...] = lower

    @pl.when(pos[0] == 1)
    def _():
        load = fetch(held_h, ext, sems.at[0])
        zero = jnp.zeros((WIN, WIN), F32)
        packet(zero, zero)
        load.wait()
        emit_rims(pos, ext, first, second)

    @pl.when(pos[0] == 0)
    def _():
        re, im, saves = run_backward(
            1, span, pos, grad, win, psi_h, probe_h, mats_h, held_h, ext_h, ext, probe, mats, psi, sems
        )
        packet(re + total[0], im + total[1])
        emit_rims(pos, ext, first, second)
        for copy in saves:
            copy.wait()


def fold_rows_kernel(pos, ext_h, row1, row2, first, second, outer, sems):
    loads = [
        fetch(ext_h.at[:, :, pl.ds(64, 128), pl.ds(0, 128)], outer.at[0], sems.at[0]),
        fetch(ext_h.at[:, :, pl.ds(64, 128), pl.ds(384, 128)], outer.at[1], sems.at[1]),
    ]
    for copy in loads:
        copy.wait()
    even = pos[1] == 0
    low = pos[2] * 64
    strip_l = join(roll_half(outer[0, 0]), outer[0, 1])
    strip_r = join(outer[1, 0], roll_half(outer[1, 1]))

    def put(out, strip, lanes):
        out[...] = strip
        for ref, start in ((row1, 64 - low), (row2, low)):
            rows = pl.ds(pl.multiple_of(start, 64), 64)
            out[:, rows, :] = out[:, rows, :] + ref[:, :, lanes]

    @pl.when(even)
    def _():
        put(first, strip_r, slice(640, 768))
        put(second, strip_l, slice(512, 640))

    @pl.when(jnp.logical_not(even))
    def _():
        put(first, strip_l, slice(512, 640))
        put(second, strip_r, slice(640, 768))


def fold_kernel(pos, ext_h, row1, row2, col1, col2, out, sems):
    fetch(ext_h.at[:, :, pl.ds(64, 128), pl.ds(128, 256)], out, sems.at[0]).wait()
    even = pos[1] == 0
    low = pos[2] * 64
    for ref, start in ((row1, 64 - low), (row2, low)):
        rows = pl.ds(pl.multiple_of(start, 64), 64)
        out[0, :, rows, :] = out[0, :, rows, :] + ref[:, :, 0:256]
        out[1, :, rows, :] = out[1, :, rows, :] + ref[:, :, 256:512]

    def columns(from_left, from_right):
        zero = jnp.zeros(from_left.shape, F32)
        out[0, :, :, :128] = out[0, :, :, :128] + join(from_left, zero)
        out[1, :, :, :128] = out[1, :, :, :128] + join(roll_half(from_left), zero)
        out[0, :, :, 128:] = out[0, :, :, 128:] + join(zero, roll_half(from_right))
        out[1, :, :, 128:] = out[1, :, :, 128:] + join(zero, from_right)

    @pl.when(even)
    def _():
        columns(inside(pos, col2[...]), col1[...])

    @pl.when(jnp.logical_not(even))
    def _():
        columns(col1[...], inside(pos, col2[...]))


def finish_kernel(scales, pos, keep, back, probe, error):
    def put(lower, upper):
        probe[0] = lower[0:128, :] * scales[0]
        probe[1, 0:8, :] = lower[128:136, :] * scales[0]
        probe[1, 8:128, :] = upper[0:120, :] * scales[0]
        error[0, 0] = jnp.max(upper[120:128, :]) * scales[1]

    @pl.when(pos[2] == 0)
    def _():
        put(keep, back)

    @pl.when(pos[2] == 1)
    def _():
        put(back, keep)


HBM = pltpu.MemorySpace.HBM
VMEM = pltpu.MemorySpace.VMEM


def call(kernel, outs, scalars, arrays, scratch=(), flops=0, hbm=(), hbm_out=(), smem_out=(), fixed=(), aliases=None):
    outs = [jax.ShapeDtypeStruct(s, F32) for s in outs]
    moved = sum(int(np.prod(a.shape)) * 4 for a in list(arrays) + outs)
    arrays = [pltpu.with_memory_space_constraint(a, HBM) if i in fixed else a for i, a in enumerate(arrays)]
    return pl.pallas_call(
        kernel,
        out_shape=outs,
        in_specs=[pl.BlockSpec(memory_space=pltpu.SMEM)] * len(scalars)
        + [pl.BlockSpec(memory_space=HBM if i in hbm else VMEM) for i in range(len(arrays))],
        out_specs=[
            pl.BlockSpec(memory_space=HBM if i in hbm_out else pltpu.SMEM if i in smem_out else VMEM)
            for i in range(len(outs))
        ],
        scratch_shapes=list(scratch),
        input_output_aliases=aliases or {},
        compiler_params=pltpu.CompilerParams(vmem_limit_bytes=VMEM_LIMIT),
        cost_estimate=pl.CostEstimate(flops=flops, bytes_accessed=moved, transcendentals=0),
    )(*scalars, *arrays)


def swap(value, axis):
    pairs = [(i, i ^ 1) for i in range(lax.axis_size(axis))]
    return lax.ppermute(value, axis, pairs)


def swap_odd_ring(value, axis):
    size = lax.axis_size(axis)
    return lax.ppermute(value, axis, [(i, (((i - 1) % size) ^ 1) + 1 if i not in (0, size - 1) else size - 1 - i) for i in range(size)])


def swap_odd(value, axis):
    size = lax.axis_size(axis)
    return lax.ppermute(value, axis, [(i, ((i - 1) ^ 1) + 1) for i in range(1, size - 1)])


AXES = ("sx", "sy", "depth")


def ring_sum(value, sizes, turn):
    rows, cols, depth = sizes

    def flat(a, b, d):
        return (a * cols + b) * depth + d

    got = []
    for step in (1, 2, 3):
        pairs = [
            (flat(a, b, d), flat(*turn(a, b, d, step))) for a in range(rows) for b in range(cols) for d in range(depth)
        ]
        got.append(lax.ppermute(value, AXES, pairs))
    return (value + got[1]) + (got[0] + got[2])


def turn_x(a, b, d, step):
    return a, b // 4 * 4 + (b + step) % 4, d


def turn_z(a, b, d, step):
    return a, (b // 4 + step) % 4 * 4 + b % 4, d


def turn_y(a, b, d, step):
    y = (a // 2 * 2 + d + step) % 4
    return y // 2 * 2 + a % 2, b, y % 2


def local(probe_wave, transmission, scan_offsets, pattern_shifts, patterns):
    slabs, rows, cols = transmission.shape[1:]
    count = scan_offsets.shape[2]
    measured = patterns.reshape(count, WIN, WIN)
    steps, exits = constants()
    core = lax.axis_index("sx") % 2
    column = lax.axis_index("sy")
    edge_column = (column == 0) | (column == lax.axis_size("sy") - 1)
    where = jnp.stack([lax.axis_index("depth"), column % 2, core, edge_column.astype(jnp.int32)]).astype(jnp.int32)
    pos = jnp.concatenate([where, scan_offsets.reshape(-1), pattern_shifts.reshape(-1)])
    sizes = (lax.axis_size("sx"), lax.axis_size("sy"), lax.axis_size("depth"))

    tile = (2, slabs, rows, cols)
    strip = (slabs, rows, 128)
    rim = (slabs, HALF, 768)
    side = (2, slabs, HALF, cols)
    corner = (slabs, HALF, 256)
    field = (count // 2, 2, WIN, WIN)
    inner = (slabs - 1,) + field
    ext = (2, slabs, rows + 2 * HALF + 8, 512)
    step_flops = 3 * 2 * 256 * 256 * WIN * count

    def vmem(shape, dtype=F32):
        return pltpu.VMEM(shape, dtype)

    def sems(n):
        return pltpu.SemaphoreType.DMA((n,))

    mats = vmem(steps.shape, BF16)
    probe = vmem(probe_wave.shape)

    col1, col2, row1, row2 = call(
        pack_kernel, [strip, strip, side, side], [where], [transmission], [vmem(tile), sems(1)], hbm=(0,), fixed=(0,)
    )
    col1, col2 = swap(col1, "sy"), swap_odd_ring(col2, "sy")
    row1, row2 = swap(row1, "sx"), swap_odd(row2, "sx")
    crn1, crn2 = call(pack_corners_kernel, [corner, corner], [where], [col1, col2])
    crn1, crn2 = swap(crn1, "sx"), swap_odd(crn2, "sx")
    spans = (tuple(range(count // 2)), tuple(range(count // 2, count)))
    assembly = [vmem(ext)]
    parts = [vmem((2,) + strip), vmem((2,) + corner)]
    wave_a, win, psi_a = call(
        functools.partial(forward_first_kernel, spans),
        [field, (slabs, count, 2, WIN, WIN), inner],
        [pos],
        [probe_wave, transmission, col1, col2, row1, row2, crn1, crn2, steps],
        [vmem(ext), probe, mats, vmem(inner)] + parts + [sems(slabs + 8)],
        slabs * step_flops,
        hbm=tuple(range(9)),
        hbm_out=(2,),
        fixed=(0, 1, 8),
    )
    wave_a = lax.ppermute(wave_a, "depth", [(0, 1)])
    wave_b, psi_b = call(
        functools.partial(forward_second_kernel, spans),
        [field, inner],
        [pos],
        [probe_wave, win, steps],
        [probe, mats, vmem(inner), sems(slabs + 8)],
        slabs * step_flops,
        hbm=(0, 2),
        hbm_out=(1,),
        fixed=(0, 2),
    )
    wave_b = lax.ppermute(wave_b, "depth", [(0, 1)])
    (win1,) = call(
        functools.partial(cut_kernel, count),
        [(slabs, count, 2, WIN, WIN)],
        [pos],
        [transmission, col1, col2, row1, row2, crn1, crn2],
        assembly + parts + [sems(7)],
        0,
        hbm=tuple(range(7)),
        fixed=(0,),
    )
    half = (len(spans[0]), WIN, WIN)
    grad_a, error, edge = call(
        functools.partial(middle_first_kernel, count, spans[0]),
        [field, (8, 128), ext],
        [pos],
        [wave_a, win1, measured, steps, exits],
        [vmem(ext), vmem(inner), vmem(half), mats, vmem(exits.shape, BF16), sems(slabs + 3)],
        2 * slabs * step_flops,
        hbm=(2, 3, 4),
        hbm_out=(2,),
        fixed=(2, 3, 4),
    )
    grad_a = lax.ppermute(grad_a, "depth", [(1, 0)])
    grad_b, error, edge = call(
        functools.partial(middle_second_kernel, count, spans[1]),
        [field, (8, 128), ext],
        [pos],
        [wave_b, win1, measured, steps, exits, edge, error],
        [vmem(ext), vmem(inner), vmem(half), mats, vmem(exits.shape, BF16), sems(2 * slabs + 3)],
        2 * slabs * step_flops,
        hbm=(2, 3, 4, 5),
        hbm_out=(2,),
        fixed=(2, 3, 4),
        aliases={6: 2},
    )
    grad_b = lax.ppermute(grad_b, "depth", [(1, 0)])
    total, edge = call(
        functools.partial(backward_first_kernel, spans[0]),
        [(2, WIN, WIN), ext],
        [pos],
        [grad_a, win, psi_a, probe_wave, steps, edge],
        [vmem(ext), probe, mats, vmem(inner), sems(slabs + 3)],
        slabs * step_flops,
        hbm=(2, 3, 4, 5),
        hbm_out=(1,),
        fixed=(3, 4),
        aliases={6: 1},
    )
    part, other, edge, row1, row2 = call(
        functools.partial(backward_second_kernel, spans[1]),
        [(136, WIN), (136, WIN), ext, rim, rim],
        [pos],
        [grad_b, win, psi_b, probe_wave, steps, edge, error, total],
        [vmem(ext), probe, mats, vmem(inner), sems(2 * slabs + 3)],
        slabs * step_flops,
        hbm=(2, 3, 4, 5),
        hbm_out=(2,),
        fixed=(3, 4),
        aliases={6: 2},
    )
    row1, row2 = swap(row1, "sx"), swap_odd(row2, "sx")
    part = part + swap(other, "sx")
    part = ring_sum(part, sizes, turn_x)
    part, row1, row2 = lax.optimization_barrier((part, row1, row2))
    col1, col2 = call(
        fold_rows_kernel, [strip, strip], [where], [edge, row1, row2],
        [vmem((2, 2) + strip), sems(2)], hbm=(0,),
    )
    part, col1, col2 = lax.optimization_barrier((part, col1, col2))
    col1, col2 = swap(col1, "sy"), swap_odd_ring(col2, "sy")
    part = ring_sum(part, sizes, turn_z)
    part, col1, col2 = lax.optimization_barrier((part, col1, col2))
    (out,) = call(fold_kernel, [tile], [where], [edge, row1, row2, col1, col2], [sems(1)], hbm=(0,))
    part = ring_sum(part, sizes, turn_y)
    other = swap(part, "sx")
    positions = count * sizes[0] * sizes[1]
    scales = jnp.array([1.0 / positions, 1.0 / (positions * WIN * WIN)], F32)
    probe_grad, error = call(finish_kernel, [(2, WIN, WIN), (1, 1)], [scales, where], [part, other], smem_out=(1,))
    return out, probe_grad, error.reshape(())


def solution(mesh):
    in_specs = (
        P(),
        P(None, "depth", "sx", "sy"),
        P("sx", "sy", None, None),
        P("sx", "sy", None, None),
        P("sx", "sy", None, None, None),
    )
    out_specs = (P(None, "depth", "sx", "sy"), P(), P())
    return jax.shard_map(local, mesh=mesh, in_specs=in_specs, out_specs=out_specs, check_vma=False)
```

```python
import functools

import jax
import jax.numpy as jnp
import numpy as np
from jax import lax
from jax.experimental import pallas as pl
from jax.experimental.pallas import tpu as pltpu
from jax.sharding import PartitionSpec as P


FRESNEL = 12.0
WIN = 128
HALF = 64
TALL = WIN + 8
LEAD = 5
F32 = jnp.float32
BF16 = jnp.bfloat16
VMEM_LIMIT = 16 * 1024 * 1024


def tables():
    n = np.arange(WIN)
    fourier = np.exp(-2j * np.pi * (np.outer(n, n) % WIN) / WIN) / np.sqrt(WIN)
    freq = np.where(n < WIN // 2, n, n - WIN) / WIN
    phase = np.exp(-1j * FRESNEL * freq * freq)
    prop = fourier.conj() @ (phase[:, None] * fourier)
    exit_left = fourier @ prop
    exit_right = prop @ fourier
    return prop, exit_left, exit_right


def right_block(m):
    return np.block([[m.real, m.imag], [-m.imag, m.real]])


def left_block(m):
    return np.block([[m.real, -m.imag], [m.imag, m.real]])


def halves(m):
    m = m.astype(np.float32)
    hi = m.astype(jnp.bfloat16)
    lo = (m - hi.astype(np.float32)).astype(jnp.bfloat16)
    return np.stack([hi, lo])


def constants():
    prop, exit_left, exit_right = tables()
    steps = halves(right_block(prop))
    exits = np.stack([halves(right_block(exit_right)), halves(left_block(exit_left))])
    return jnp.asarray(steps), jnp.asarray(exits)


def step_pair(mats):
    right = (mats[0], mats[1])

    def other(m):
        top = jnp.concatenate([m[:WIN, :WIN], m[WIN:, :WIN]], axis=1)
        bottom = jnp.concatenate([m[:WIN, WIN:], m[WIN:, WIN:]], axis=1)
        return jnp.concatenate([top, bottom], axis=0)

    return right, (other(right[0]), other(right[1]))


def split(x):
    hi = x.astype(BF16)
    return hi, (x - hi.astype(F32)).astype(BF16)


def mm(a, b):
    return jnp.dot(a, b, preferred_element_type=F32)


def mm3(a, b):
    return mm(jnp.concatenate([a[0], a[1], a[0]], axis=1), jnp.concatenate([b[0], b[0], b[1]], axis=0))


def apply_both(fields, right, left):
    rows = jnp.concatenate([jnp.concatenate([re, im], axis=1) for re, im in fields], axis=0)
    z = mm3(split(rows), right)
    cols = jnp.concatenate(
        [
            jnp.concatenate([z[p * WIN : (p + 1) * WIN, :WIN], z[p * WIN : (p + 1) * WIN, WIN:]], axis=0)
            for p in range(len(fields))
        ],
        axis=1,
    )
    y = mm3(left, split(cols))
    return [
        (y[:WIN, p * WIN : (p + 1) * WIN], y[WIN:, p * WIN : (p + 1) * WIN]) for p in range(len(fields))
    ]


def times(a, b):
    return a[0] * b[0] - a[1] * b[1], a[0] * b[1] + a[1] * b[0]


def conj_times(a, b):
    return a[0] * b[0] + a[1] * b[1], a[0] * b[1] - a[1] * b[0]


def pair(ref, i):
    return ref[i, 0], ref[i, 1]


def roll_half(x):
    return pltpu.roll(x, HALF, axis=x.ndim - 1)


def join(low, high):
    lane = lax.broadcasted_iota(jnp.int32, low.shape, low.ndim - 1)
    return jnp.where(lane < HALF, low, high)


def fetch(src, dst, sem):
    copy = pltpu.make_async_copy(src, dst, sem)
    copy.start()
    return copy


def pack_kernel(pos, source, col1, col2, row1, row2, tile, sems):
    low = pos[2] * 64
    loads = [
        fetch(source.at[:, :, :, pl.ds(0, 128)], tile.at[0], sems.at[0]),
        fetch(source.at[:, :, :, pl.ds(128, 128)], tile.at[1], sems.at[1]),
        fetch(source.at[:, :, pl.ds(pl.multiple_of(64 - low, 64), 64), :], row1, sems.at[2]),
        fetch(source.at[:, :, pl.ds(pl.multiple_of(low, 64), 64), :], row2, sems.at[3]),
    ]
    even = pos[1] == 0
    loads[0].wait()
    left = join(tile[0, 0], roll_half(tile[0, 1]))

    @pl.when(even)
    def _():
        col2[...] = left

    @pl.when(jnp.logical_not(even))
    def _():
        col1[...] = left

    loads[1].wait()
    right = join(roll_half(tile[1, 0]), tile[1, 1])

    @pl.when(even)
    def _():
        col1[...] = right

    @pl.when(jnp.logical_not(even))
    def _():
        col2[...] = right

    loads[2].wait()
    loads[3].wait()


def pack_corners_kernel(pos, col1, col2, first, second):
    even = pos[1] == 0
    low = pos[2] * 64
    for out, start in ((first, 64 - low), (second, low)):
        rows = pl.ds(pl.multiple_of(start, 64), 64)
        ring = inside(pos, col2[:, rows, :])

        @pl.when(even)
        def _():
            out[:, :, :128] = ring
            out[:, :, 128:] = col1[:, rows, :]

        @pl.when(jnp.logical_not(even))
        def _():
            out[:, :, :128] = col1[:, rows, :]
            out[:, :, 128:] = ring


def inside(pos, value, flag=3):
    return jnp.where(pos[flag] == 1, 0.0, value)


def load_window(ext, c, k, row, block, shift):
    base = pl.multiple_of(row // 8 * 8, 8)
    wide = ext[c, k, pl.ds(base, TALL), pl.ds(pl.multiple_of(block * 128, 128), 256)]
    wide = pltpu.roll(wide, (256 - shift) & 255, axis=1)[:, :WIN]
    return pltpu.roll(wide, (TALL - row % 8) % TALL, axis=0)[:WIN]


def place(pos, p):
    row = pos[LEAD + 2 * p] + HALF
    col = pos[LEAD + 1 + 2 * p] + 128
    return row, col // 128, col % 128


def assemble(pos, tile, cols_h, rows_h, corners_h, ext, cols, corners, sems):
    odd_row = pos[2]
    starts = (pl.multiple_of(192 * (1 - odd_row), 64), pl.multiple_of(192 * odd_row, 64))
    first = pos[1]
    near = [
        fetch(cols_h[0], cols.at[1 - first], sems.at[0]),
        fetch(cols_h[1], cols.at[first], sems.at[1]),
        fetch(corners_h[0], corners.at[0], sems.at[2]),
        fetch(corners_h[1], corners.at[1], sems.at[3]),
    ]
    far = [
        fetch(tile, ext.at[:, :, pl.ds(64, 128), pl.ds(128, 256)], sems.at[4]),
        fetch(rows_h[0], ext.at[:, :, pl.ds(starts[0], 64), pl.ds(128, 256)], sems.at[5]),
        fetch(rows_h[1], ext.at[:, :, pl.ds(starts[1], 64), pl.ds(128, 256)], sems.at[6]),
    ]
    for copy in near:
        copy.wait()

    def sides(rows, left, right):
        ext[0, :, rows, 0:128] = roll_half(left)
        ext[1, :, rows, 0:128] = left
        ext[0, :, rows, 384:512] = right
        ext[1, :, rows, 384:512] = roll_half(right)

    cols[first] = inside(pos, cols[first])
    sides(slice(64, 192), cols[0], cols[1])
    corners[1] = inside(pos, corners[1], 4)
    for i in range(2):
        sides(pl.ds(starts[i], 64), corners[i, :, :, :128], corners[i, :, :, 128:])
    for copy in far:
        copy.wait()


def cut_window(pos, ext, p, k, win):
    row, block, shift = place(pos, p)
    win[k, p, 0] = load_window(ext, 0, k, row, block, shift) + 1.0
    win[k, p, 1] = load_window(ext, 1, k, row, block, shift)


def run_forward(span, probe, mats, win, wave, psi_h, psi, sems, after):
    slabs = win.shape[0]
    right, left = step_pair(mats)
    fields = [(probe[0], probe[1])] * len(span)
    saves = []
    for k in range(slabs):
        if k:
            for i in range(len(span)):
                psi[k - 1, i, 0], psi[k - 1, i, 1] = fields[i]
            saves.append(fetch(psi.at[k - 1], psi_h.at[k - 1], sems.at[8 + k]))
        fields = apply_both([times(fields[i], pair(win.at[k], p)) for i, p in enumerate(span)], right, left)
        after(k)
    for i in range(len(span)):
        wave[i, 0], wave[i, 1] = fields[i]
    for copy in saves:
        copy.wait()


def forward_first_kernel(
    spans, pos, probe_h, tile, col1_h, col2_h, row1, row2, crn1_h, crn2_h, mats_h,
    wave, win, psi_h, ext, probe, mats, psi, cols, corners, sems,
):
    slabs = tile.shape[1]

    @pl.when(pos[0] == 0)
    def _():
        loads = [fetch(probe_h, probe, sems.at[7]), fetch(mats_h, mats, sems.at[8])]
        assemble(pos, tile, (col1_h, col2_h), (row1, row2), (crn1_h, crn2_h), ext, cols, corners, sems)
        for copy in loads:
            copy.wait()
        for k in range(slabs):
            for p in spans[0]:
                cut_window(pos, ext, p, k, win)

        def after(k):
            for p in spans[1]:
                cut_window(pos, ext, p, k, win)

        run_forward(spans[0], probe, mats, win, wave, psi_h, psi, sems, after)


def forward_second_kernel(spans, pos, probe_h, win, mats_h, wave, psi_h, probe, mats, psi, sems):
    @pl.when(pos[0] == 0)
    def _():
        loads = [fetch(probe_h, probe, sems.at[7]), fetch(mats_h, mats, sems.at[8])]
        for copy in loads:
            copy.wait()
        run_forward(spans[1], probe, mats, win, wave, psi_h, psi, sems, lambda k: None)


def cut_kernel(count, pos, tile, col1_h, col2_h, row1, row2, crn1_h, crn2_h, win, ext, cols, corners, sems):
    slabs = tile.shape[1]

    @pl.when(pos[0] == 1)
    def _():
        assemble(pos, tile, (col1_h, col2_h), (row1, row2), (crn1_h, crn2_h), ext, cols, corners, sems)

        @pl.loop(0, count)
        def _(p):
            for k in range(slabs):
                cut_window(pos, ext, p, k, win)


def add_window(ext, c, k, row, block, shift, piece):
    tall = pltpu.roll(jnp.concatenate([piece, jnp.zeros((TALL - WIN, WIN), F32)], axis=0), row % 8, axis=0)
    wide = pltpu.roll(jnp.concatenate([tall, jnp.zeros_like(tall)], axis=1), shift, axis=1)
    base = pl.multiple_of(row // 8 * 8, 8)
    at = (c, k, pl.ds(base, TALL), pl.ds(pl.multiple_of(block * 128, 128), 256))
    ext[at] = ext[at] + wide


def strips(ext, rows):
    left = join(roll_half(ext[0, :, rows, 0:128]), ext[1, :, rows, 0:128])
    right = join(ext[0, :, rows, 384:512], roll_half(ext[1, :, rows, 384:512]))
    return left, right


def emit_rims(pos, ext, first, second):
    def rim(out, start):
        rows = pl.ds(pl.multiple_of(start, 64), 64)
        out[:, :, 0:256] = ext[0, :, rows, 128:384]
        out[:, :, 256:512] = ext[1, :, rows, 128:384]
        out[:, :, 512:640], out[:, :, 640:768] = strips(ext, rows)

    odd_row = pos[2]
    rim(first, 192 * (1 - odd_row))
    rim(second, 192 * odd_row)


def backward_slabs(span, pos, grads, win, incident, ext, right, left, ext_h, sems, loads):
    slabs = win.shape[0]
    saves = []
    for k in reversed(range(slabs)):
        if grads[0] == "exit":
            fields = grads[1]
        else:
            fields = apply_both(grads[1], left, right)
        if loads:
            loads[k].wait()
        nxt = []
        for i, p in enumerate(span):
            row, block, shift = place(pos, p)
            piece = conj_times(incident(k, i), fields[i])
            add_window(ext, 0, k, row, block, shift, piece[0])
            add_window(ext, 1, k, row, block, shift, piece[1])
            nxt.append(conj_times(pair(win.at[k], p), fields[i]))
        saves.append(fetch(ext.at[:, k], ext_h.at[:, k], sems.at[k]))
        grads = ("inner", nxt)
    return grads[1], saves


def start_ext(group, ext, held_h, sems, at, slabs):
    if group == 0:
        ext[...] = jnp.zeros_like(ext)
        return None
    return [fetch(held_h.at[:, k], ext.at[:, k], sems.at[at + k]) for k in range(slabs)]


def middle_body(
    group, count, span, pos, wave, win, measured_h, mats_h, exits_h, held_h, before,
    grad, error, ext_h, ext, psi, measured, mats, exits, sems,
):
    slabs = win.shape[0]
    extra = slabs + 3

    @pl.when(pos[0] == 0)
    def _():
        error[...] = jnp.zeros_like(error)

    @pl.when(pos[0] == 1)
    def _():
        loads = [
            fetch(mats_h, mats, sems.at[slabs]),
            fetch(exits_h, exits, sems.at[slabs + 1]),
            fetch(measured_h.at[pl.ds(span[0], len(span))], measured, sems.at[slabs + 2]),
        ]
        held = start_ext(group, ext, held_h, sems, extra, slabs)
        loads[0].wait()
        right, left = step_pair(mats)
        fields = [pair(wave, i) for i in range(len(span))]
        for k in range(slabs):
            if k:
                for i in range(len(span)):
                    psi[k - 1, i, 0], psi[k - 1, i, 1] = fields[i]
            entering = [times(fields[i], pair(win.at[k], p)) for i, p in enumerate(span)]
            if k < slabs - 1:
                fields = apply_both(entering, right, left)
            else:
                loads[1].wait()
                exit_right = (exits[0, 0], exits[0, 1])
                exit_left = (exits[1, 0], exits[1, 1])
                fields = apply_both(entering, exit_right, exit_left)
        loads[2].wait()
        total = jnp.zeros((8, 128), F32)
        far = []
        for i, p in enumerate(span):
            at = LEAD + 2 * count + 2 * p
            target = pltpu.roll(measured[i], (128 - pos[at]) & 127, axis=0)
            target = pltpu.roll(target, (128 - pos[at + 1]) & 127, axis=1)
            re, im = fields[i]
            residual = re * re + im * im - target
            total = total + jnp.sum((residual * residual).reshape(16, 8, 128), axis=0)
            twice = 2.0 * residual
            far.append((twice * re, twice * im))
        part = jnp.full((8, 128), 0.5 * jnp.sum(total), F32)
        error[...] = part if group == 0 else before[...] + part
        entry = apply_both(far, exit_left, exit_right)

        def incident(k, i):
            return pair(wave, i) if k == 0 else pair(psi.at[k - 1], i)

        out, saves = backward_slabs(span, pos, ("exit", entry), win, incident, ext, right, left, ext_h, sems, held)
        for i in range(len(span)):
            grad[i, 0], grad[i, 1] = out[i]
        for copy in saves:
            copy.wait()


def middle_first_kernel(count, span, pos, wave, win, measured_h, mats_h, exits_h, *rest):
    middle_body(0, count, span, pos, wave, win, measured_h, mats_h, exits_h, None, None, *rest)


def middle_second_kernel(count, span, pos, wave, win, measured_h, mats_h, exits_h, held_h, before, *rest):
    middle_body(1, count, span, pos, wave, win, measured_h, mats_h, exits_h, held_h, before, *rest)


def run_backward(group, span, pos, grad, win, psi_h, probe_h, mats_h, held_h, ext_h, ext, probe, mats, psi, sems):
    slabs = win.shape[0]
    loads = [
        fetch(mats_h, mats, sems.at[slabs]),
        fetch(psi_h, psi, sems.at[slabs + 1]),
        fetch(probe_h, probe, sems.at[slabs + 2]),
    ]
    held = start_ext(group, ext, held_h, sems, slabs + 3, slabs)
    loads[0].wait()
    right, left = step_pair(mats)

    def incident(k, i):
        if i == 0 and k == slabs - 1:
            loads[1].wait()
        if i == 0 and k == 0:
            loads[2].wait()
        return (probe[0], probe[1]) if k == 0 else pair(psi.at[k - 1], i)

    grads = ("inner", [pair(grad, i) for i in range(len(span))])
    out, saves = backward_slabs(span, pos, grads, win, incident, ext, right, left, ext_h, sems, held)
    re = sum(o[0] for o in out[1:]) + out[0][0]
    im = sum(o[1] for o in out[1:]) + out[0][1]
    return re, im, saves


def backward_first_kernel(
    span, pos, grad, win, psi_h, probe_h, mats_h, held_h, total, ext_h, ext, probe, mats, psi, sems
):
    @pl.when(pos[0] == 0)
    def _():
        re, im, saves = run_backward(
            0, span, pos, grad, win, psi_h, probe_h, mats_h, held_h, ext_h, ext, probe, mats, psi, sems
        )
        total[0] = re
        total[1] = im
        for copy in saves:
            copy.wait()


def backward_second_kernel(
    span, pos, grad, win, psi_h, probe_h, mats_h, held_h, error, total,
    keep, send, ext_h, first, second, ext, probe, mats, psi, sems,
):
    def packet(re, im):
        upper = jnp.concatenate([im[8:], error[...]], axis=0)
        lower = jnp.concatenate([re, im[:8]], axis=0)

        @pl.when(pos[2] == 0)
        def _():
            keep[...] = lower
            send[0:128, :] = upper
            send[128:136, :] = jnp.zeros((8, 128), F32)

        @pl.when(pos[2] == 1)
        def _():
            keep[0:128, :] = upper
            keep[128:136, :] = jnp.zeros((8, 128), F32)
            send[...] = lower

    @pl.when(pos[0] == 1)
    def _():
        load = fetch(held_h, ext, sems.at[0])
        zero = jnp.zeros((WIN, WIN), F32)
        packet(zero, zero)
        load.wait()
        emit_rims(pos, ext, first, second)

    @pl.when(pos[0] == 0)
    def _():
        re, im, saves = run_backward(
            1, span, pos, grad, win, psi_h, probe_h, mats_h, held_h, ext_h, ext, probe, mats, psi, sems
        )
        packet(re + total[0], im + total[1])
        emit_rims(pos, ext, first, second)
        for copy in saves:
            copy.wait()


def fold_rows_kernel(pos, ext_h, row1, row2, first, second, outer, sems):
    loads = [
        fetch(ext_h.at[:, :, pl.ds(64, 128), pl.ds(0, 128)], outer.at[0], sems.at[0]),
        fetch(ext_h.at[:, :, pl.ds(64, 128), pl.ds(384, 128)], outer.at[1], sems.at[1]),
    ]
    for copy in loads:
        copy.wait()
    even = pos[1] == 0
    low = pos[2] * 64
    strip_l = join(roll_half(outer[0, 0]), outer[0, 1])
    strip_r = join(outer[1, 0], roll_half(outer[1, 1]))

    def put(out, strip, lanes):
        out[...] = strip
        for ref, start in ((row1, 64 - low), (row2, low)):
            rows = pl.ds(pl.multiple_of(start, 64), 64)
            out[:, rows, :] = out[:, rows, :] + ref[:, :, lanes]

    @pl.when(even)
    def _():
        put(first, strip_r, slice(640, 768))
        put(second, strip_l, slice(512, 640))

    @pl.when(jnp.logical_not(even))
    def _():
        put(first, strip_l, slice(512, 640))
        put(second, strip_r, slice(640, 768))


def fold_kernel(pos, ext_h, row1, row2, col1, col2, out, sems):
    fetch(ext_h.at[:, :, pl.ds(64, 128), pl.ds(128, 256)], out, sems.at[0]).wait()
    even = pos[1] == 0
    low = pos[2] * 64
    for ref, start in ((row1, 64 - low), (row2, low)):
        rows = pl.ds(pl.multiple_of(start, 64), 64)
        out[0, :, rows, :] = out[0, :, rows, :] + ref[:, :, 0:256]
        out[1, :, rows, :] = out[1, :, rows, :] + ref[:, :, 256:512]

    def columns(from_left, from_right):
        zero = jnp.zeros(from_left.shape, F32)
        out[0, :, :, :128] = out[0, :, :, :128] + join(from_left, zero)
        out[1, :, :, :128] = out[1, :, :, :128] + join(roll_half(from_left), zero)
        out[0, :, :, 128:] = out[0, :, :, 128:] + join(zero, roll_half(from_right))
        out[1, :, :, 128:] = out[1, :, :, 128:] + join(zero, from_right)

    @pl.when(even)
    def _():
        columns(inside(pos, col2[...]), col1[...])

    @pl.when(jnp.logical_not(even))
    def _():
        columns(col1[...], inside(pos, col2[...]))


def finish_kernel(scales, pos, keep, back, probe, error):
    def put(lower, upper):
        probe[0] = lower[0:128, :] * scales[0]
        probe[1, 0:8, :] = lower[128:136, :] * scales[0]
        probe[1, 8:128, :] = upper[0:120, :] * scales[0]
        error[0, 0] = jnp.max(upper[120:128, :]) * scales[1]

    @pl.when(pos[2] == 0)
    def _():
        put(keep, back)

    @pl.when(pos[2] == 1)
    def _():
        put(back, keep)


HBM = pltpu.MemorySpace.HBM
VMEM = pltpu.MemorySpace.VMEM


def call(kernel, outs, scalars, arrays, scratch=(), flops=0, hbm=(), hbm_out=(), smem_out=(), fixed=(), aliases=None):
    outs = [jax.ShapeDtypeStruct(s, F32) for s in outs]
    moved = sum(int(np.prod(a.shape)) * 4 for a in list(arrays) + outs)
    arrays = [pltpu.with_memory_space_constraint(a, HBM) if i in fixed else a for i, a in enumerate(arrays)]
    return pl.pallas_call(
        kernel,
        out_shape=outs,
        in_specs=[pl.BlockSpec(memory_space=pltpu.SMEM)] * len(scalars)
        + [pl.BlockSpec(memory_space=HBM if i in hbm else VMEM) for i in range(len(arrays))],
        out_specs=[
            pl.BlockSpec(memory_space=HBM if i in hbm_out else pltpu.SMEM if i in smem_out else VMEM)
            for i in range(len(outs))
        ],
        scratch_shapes=list(scratch),
        input_output_aliases=aliases or {},
        compiler_params=pltpu.CompilerParams(vmem_limit_bytes=VMEM_LIMIT),
        cost_estimate=pl.CostEstimate(flops=flops, bytes_accessed=moved, transcendentals=0),
    )(*scalars, *arrays)


def swap(value, axis):
    pairs = [(i, i ^ 1) for i in range(lax.axis_size(axis))]
    return lax.ppermute(value, axis, pairs)


def closed(value, sizes, move):
    rows, cols = sizes[:2]
    pairs = [(a * cols + b, move(a, b)[0] * cols + move(a, b)[1]) for a in range(rows) for b in range(cols)]
    return lax.ppermute(value, ("sx", "sy"), pairs)


def swap_odd_columns(value, sizes):
    last = sizes[1] - 1
    return closed(value, sizes, lambda a, b: (a ^ 1, b) if b in (0, last) else (a, ((b - 1) ^ 1) + 1))


def swap_odd_rows(value, sizes):
    last = sizes[0] - 1
    return closed(value, sizes, lambda a, b: (a, b ^ 1) if a in (0, last) else (((a - 1) ^ 1) + 1, b))


def swap_odd(value, axis):
    size = lax.axis_size(axis)
    return lax.ppermute(value, axis, [(i, ((i - 1) ^ 1) + 1) for i in range(1, size - 1)])


AXES = ("sx", "sy", "depth")


def ring_sum(value, sizes, turn):
    rows, cols, depth = sizes

    def flat(a, b, d):
        return (a * cols + b) * depth + d

    got = []
    for step in (1, 2, 3):
        pairs = [
            (flat(a, b, d), flat(*turn(a, b, d, step))) for a in range(rows) for b in range(cols) for d in range(depth)
        ]
        got.append(lax.ppermute(value, AXES, pairs))
    return (value + got[1]) + (got[0] + got[2])


def turn_x(a, b, d, step):
    return a, b // 4 * 4 + (b + step) % 4, d


def turn_z(a, b, d, step):
    return a, (b // 4 + step) % 4 * 4 + b % 4, d


def turn_y(a, b, d, step):
    y = (a // 2 * 2 + d + step) % 4
    return y // 2 * 2 + a % 2, b, y % 2


def local(probe_wave, transmission, scan_offsets, pattern_shifts, patterns):
    slabs, rows, cols = transmission.shape[1:]
    count = scan_offsets.shape[2]
    measured = patterns.reshape(count, WIN, WIN)
    steps, exits = constants()
    core = lax.axis_index("sx") % 2
    column = lax.axis_index("sy")
    edge_column = (column == 0) | (column == lax.axis_size("sy") - 1)
    edge_row = (lax.axis_index("sx") == 0) | (lax.axis_index("sx") == lax.axis_size("sx") - 1)
    where = jnp.stack(
        [lax.axis_index("depth"), column % 2, core, edge_column.astype(jnp.int32), edge_row.astype(jnp.int32)]
    ).astype(jnp.int32)
    pos = jnp.concatenate([where, scan_offsets.reshape(-1), pattern_shifts.reshape(-1)])
    sizes = (lax.axis_size("sx"), lax.axis_size("sy"), lax.axis_size("depth"))

    tile = (2, slabs, rows, cols)
    strip = (slabs, rows, 128)
    rim = (slabs, HALF, 768)
    side = (2, slabs, HALF, cols)
    corner = (slabs, HALF, 256)
    field = (count // 2, 2, WIN, WIN)
    inner = (slabs - 1,) + field
    ext = (2, slabs, rows + 2 * HALF + 8, 512)
    step_flops = 3 * 2 * 256 * 256 * WIN * count

    def vmem(shape, dtype=F32):
        return pltpu.VMEM(shape, dtype)

    def sems(n):
        return pltpu.SemaphoreType.DMA((n,))

    mats = vmem(steps.shape, BF16)
    probe = vmem(probe_wave.shape)

    col1, col2, row1, row2 = call(
        pack_kernel, [strip, strip, side, side], [where], [transmission], [vmem((2, 2) + strip), sems(4)], hbm=(0,), fixed=(0,)
    )
    col1, col2 = swap(col1, "sy"), swap_odd_columns(col2, sizes)
    row1, row2 = swap(row1, "sx"), swap_odd(row2, "sx")
    crn1, crn2 = call(pack_corners_kernel, [corner, corner], [where], [col1, col2])
    crn1, crn2 = swap(crn1, "sx"), swap_odd_rows(crn2, sizes)
    spans = (tuple(range(count // 2)), tuple(range(count // 2, count)))
    assembly = [vmem(ext)]
    parts = [vmem((2,) + strip), vmem((2,) + corner)]
    wave_a, win, psi_a = call(
        functools.partial(forward_first_kernel, spans),
        [field, (slabs, count, 2, WIN, WIN), inner],
        [pos],
        [probe_wave, transmission, col1, col2, row1, row2, crn1, crn2, steps],
        [vmem(ext), probe, mats, vmem(inner)] + parts + [sems(slabs + 8)],
        slabs * step_flops,
        hbm=tuple(range(9)),
        hbm_out=(2,),
        fixed=(0, 1, 8),
    )
    wave_a = lax.ppermute(wave_a, "depth", [(0, 1), (1, 0)])
    wave_b, psi_b = call(
        functools.partial(forward_second_kernel, spans),
        [field, inner],
        [pos],
        [probe_wave, win, steps],
        [probe, mats, vmem(inner), sems(slabs + 8)],
        slabs * step_flops,
        hbm=(0, 2),
        hbm_out=(1,),
        fixed=(0, 2),
    )
    wave_b = lax.ppermute(wave_b, "depth", [(0, 1)])
    (win1,) = call(
        functools.partial(cut_kernel, count),
        [(slabs, count, 2, WIN, WIN)],
        [pos],
        [transmission, col1, col2, row1, row2, crn1, crn2],
        assembly + parts + [sems(7)],
        0,
        hbm=tuple(range(7)),
        fixed=(0,),
    )
    half = (len(spans[0]), WIN, WIN)
    grad_a, error, edge = call(
        functools.partial(middle_first_kernel, count, spans[0]),
        [field, (8, 128), ext],
        [pos],
        [wave_a, win1, measured, steps, exits],
        [vmem(ext), vmem(inner), vmem(half), mats, vmem(exits.shape, BF16), sems(slabs + 3)],
        2 * slabs * step_flops,
        hbm=(2, 3, 4),
        hbm_out=(2,),
        fixed=(2, 3, 4),
    )
    grad_a = lax.ppermute(grad_a, "depth", [(1, 0)])
    grad_b, error, edge = call(
        functools.partial(middle_second_kernel, count, spans[1]),
        [field, (8, 128), ext],
        [pos],
        [wave_b, win1, measured, steps, exits, edge, error],
        [vmem(ext), vmem(inner), vmem(half), mats, vmem(exits.shape, BF16), sems(2 * slabs + 3)],
        2 * slabs * step_flops,
        hbm=(2, 3, 4, 5),
        hbm_out=(2,),
        fixed=(2, 3, 4),
        aliases={6: 2},
    )
    grad_b = lax.ppermute(grad_b, "depth", [(1, 0), (0, 1)])
    total, edge = call(
        functools.partial(backward_first_kernel, spans[0]),
        [(2, WIN, WIN), ext],
        [pos],
        [grad_a, win, psi_a, probe_wave, steps, edge],
        [vmem(ext), probe, mats, vmem(inner), sems(slabs + 3)],
        slabs * step_flops,
        hbm=(2, 3, 4, 5),
        hbm_out=(1,),
        fixed=(3, 4),
        aliases={6: 1},
    )
    part, other, edge, row1, row2 = call(
        functools.partial(backward_second_kernel, spans[1]),
        [(136, WIN), (136, WIN), ext, rim, rim],
        [pos],
        [grad_b, win, psi_b, probe_wave, steps, edge, error, total],
        [vmem(ext), probe, mats, vmem(inner), sems(2 * slabs + 3)],
        slabs * step_flops,
        hbm=(2, 3, 4, 5),
        hbm_out=(2,),
        fixed=(3, 4),
        aliases={6: 2},
    )
    row1, row2 = swap(row1, "sx"), swap_odd(row2, "sx")
    part = part + swap(other, "sx")
    part = ring_sum(part, sizes, turn_x)
    part, row1, row2 = lax.optimization_barrier((part, row1, row2))
    col1, col2 = call(
        fold_rows_kernel, [strip, strip], [where], [edge, row1, row2],
        [vmem((2, 2) + strip), sems(2)], hbm=(0,),
    )
    part, col1, col2 = lax.optimization_barrier((part, col1, col2))
    col1, col2 = swap(col1, "sy"), swap_odd_columns(col2, sizes)
    part = ring_sum(part, sizes, turn_y)
    part, col1, col2 = lax.optimization_barrier((part, col1, col2))
    (out,) = call(fold_kernel, [tile], [where], [edge, row1, row2, col1, col2], [sems(1)], hbm=(0,))
    part = ring_sum(part, sizes, turn_z)
    other = swap(part, "sx")
    positions = count * sizes[0] * sizes[1]
    scales = jnp.array([1.0 / positions, 1.0 / (positions * WIN * WIN)], F32)
    probe_grad, error = call(finish_kernel, [(2, WIN, WIN), (1, 1)], [scales, where], [part, other], smem_out=(1,))
    return out, probe_grad, error.reshape(())


def solution(mesh):
    in_specs = (
        P(),
        P(None, "depth", "sx", "sy"),
        P("sx", "sy", None, None),
        P("sx", "sy", None, None),
        P("sx", "sy", None, None, None),
    )
    out_specs = (P(None, "depth", "sx", "sy"), P(), P())
    return jax.shard_map(local, mesh=mesh, in_specs=in_specs, out_specs=out_specs, check_vma=False)
```
